128 devices in a mesh: side: 2 (over core), grp: 8 (over x_hi, y), tp: 8 (over x_lo, z).
Axes of the slice: x: 4 (x_hi: 2, x_lo: 2; x = x_hi * 2 + x_lo), y: 4, z: 4, core: 2. Of those that a mesh axis runs over, the one named last changes fastest.
Arguments:
- queries: bfloat16 [192, 4096], P('grp', 'side'), may hold values from -6 to 6
- kv_cache: bfloat16 [192, 16, 192, 256], P('grp', ('side', 'tp')), may hold values from -6 to 6
- lengths: int32 [192], P('grp'), may hold values from 2 to 768, as said below
- out_weight: bfloat16 [4096, 2048], P(('side', 'tp')), may hold values from -1 to 1
- resid: bfloat16 [192, 2048], P('grp'), may hold values from -6 to 6
- norm_gain: float32 [2048], replicated, may hold values from 0.1 to 1.9
- expert_ids: int32 [192, 8], P('grp'), may hold values from 0 to 127, all different within a row; in each aligned block of 24 rows (0 to 23, 24 to 47, ...) at most 3 rows name the same one
- expert_gates: float32 [192, 8], P('grp'), may hold values from 0.05 to 1
- w_gate_up: bfloat16 [128, 2048, 1536], P(('side', 'grp', 'tp')), may hold values from -0.125 to 0.125
- w_down: bfloat16 [128, 768, 2048], P(('side', 'grp', 'tp')), may hold values from -0.21875 to 0.21875
Outputs:
- layer_out: bfloat16 [192, 2048], P('grp', ('side', 'tp'))
The draws below stay inside these ranges and needn't reach their ends.
Inputs may be any that keep to these rules, and one draw needn't show every extreme that they name: `lengths`: every row's cache holds at least two tokens; some row holds exactly 768. `expert_ids`: each row names 8 different experts. Among the rows of one row group no expert is named by more than 3 rows; in some group an expert is named by exactly 3.
All inputs are finite; a program needn't handle non-finite values.
Results may differ from the reference program's by a relative error of at most 0.017.
Values may be sent and summed in bfloat16 or wider, within the bound.
A program may use at most 64 MiB of HBM per device.

```python
import math
import jax
import jax.numpy as jnp
import numpy as np
from jax import lax

D = 2048
QH = 32
KVH = 4
HD = 128
FFE = 768
TOPK = 8
L = 768
ROWS_GRP = 24
EXPERTS = 128
ROWS = 192
KV_PARTS = 4
L_PART = 192
CAP = 3
N_GRP = 8


def draw_queries(key, part):
    drawn = jnp.clip(jax.random.normal(jax.random.fold_in(key, 11), (ROWS, QH, HD), jnp.float32), -6.0, 6.0)
    return drawn.reshape(ROWS, QH * HD).astype(jnp.bfloat16)


def draw_kv_cache(key, part):
    drawn = jnp.clip(jax.random.normal(jax.random.fold_in(key, 12), (ROWS, KVH * KV_PARTS, L_PART, 2 * HD), jnp.float32), -6.0, 6.0)
    return drawn.astype(jnp.bfloat16)


def draw_lengths(key, part):
    drawn_lengths = jax.random.randint(jax.random.fold_in(key, 13), (ROWS,), 2, L + 1)
    full_row = jax.random.randint(jax.random.fold_in(key, 14), (), 0, ROWS)
    return jnp.where(jnp.arange(ROWS) == full_row, L, drawn_lengths).astype(jnp.int32)


def level_of(stream_key, extent, shards, smallest, high):
    def one(position, blocks):
        heights = jax.random.uniform(jax.random.fold_in(jax.random.fold_in(stream_key, 6), position), (blocks,), jnp.float32, smallest / len(shards), high / len(shards))
        return jnp.repeat(jnp.exp(heights), extent[position] // blocks).reshape((-1,) + (1,) * (len(extent) - position - 1))

    factor_of = one(*shards[0])
    for cut in shards[1:]:
        factor_of = factor_of * one(*cut)
    return factor_of


def assign_block(stream_key, own, number, rows, number_of, top, limit, slope):
    order = jax.random.permutation(stream_key, number_of)
    crowded, usual = shares(number_of, rows * top, limit, slope, True), shares(number_of, rows * top, limit, slope, False)
    places = jnp.arange(number_of)

    def named(sizes, rotation):
        used = int((sizes > 0).sum())
        fixed = max(1, used // 4)
        shifted = fixed + (places - fixed + rotation * (used - fixed)) % max(1, number_of - fixed)
        return jnp.zeros((number_of,), jnp.int32).at[order[jnp.where(places < fixed, places, shifted)]].set(jnp.asarray(sizes, jnp.int32))

    sizes = jnp.where(number % 4 == 0, named(crowded, number // 4), named(usual, number - number // 4 - 1))
    mixed = jax.random.permutation(jax.random.fold_in(own, 3), number_of)
    source_of, taker = mixed[0:number_of // 2 * 2:2], mixed[1:number_of // 2 * 2:2]
    slack = jnp.minimum(sizes[source_of] - 1, limit - sizes[taker]) // 2
    slack = jnp.where((source_of == order[0]) | (taker == order[0]) | (sizes[taker] == 0), 0, jnp.maximum(slack, 0))
    shifted = jax.random.randint(jax.random.fold_in(own, 4), (number_of // 2,), 0, 1 << 20) % (slack + 1)
    sizes = sizes.at[source_of].add(-shifted).at[taker].add(shifted)
    members = jnp.searchsorted(jnp.cumsum(sizes), jnp.arange(rows * top), side="right").astype(jnp.int32)
    listing = members.reshape(top, rows).T
    listing = listing[jax.random.permutation(jax.random.fold_in(own, 1), rows)]
    rotation = jax.random.randint(jax.random.fold_in(own, 2), (rows, 1), 0, top)
    return jnp.take_along_axis(listing, (jnp.arange(top)[None, :] + rotation) % top, axis=1)


def shares(number_of, total, limit, slope, full):
    loads = [(1 << 20) // math.isqrt(standing ** slope) + 1 for standing in range(1, number_of + 1)]
    largest = limit if full else min(limit, max(-(-total // number_of), total * loads[0] // sum(loads)))
    least = 1 if total - largest >= number_of - 1 else 0
    holding, spare = [largest] + [least] * (number_of - 1), total - largest - least * (number_of - 1)
    while spare > 0:
        movable = [i for i in range(1, number_of) if holding[i] < largest] or [i for i in range(1, number_of) if holding[i] < limit]
        mass, left = sum([loads[i] for i in movable]), spare
        for i in movable:
            more = min(limit - holding[i], max(1, left * loads[i] // mass), spare)
            holding[i] = holding[i] + more
            spare = spare - more
    return np.array(holding)


def gaussian(stream_key, dims, width, most, pieces=(), kind=jnp.bfloat16):
    values = jax.random.normal(stream_key, dims, jnp.float32) * width
    if len(pieces) > 0:
        values = level_of(stream_key, dims, pieces, -0.22, 0.18) * values
    return jnp.clip(values, min=-most, max=most).astype(kind)


def setup_inputs(seed: int = 0) -> dict:
    arg_keys = jax.random.split(jax.random.key(seed), 11)
    queries = draw_queries(jax.random.fold_in(arg_keys[10], 71), 0)
    kv_cache = draw_kv_cache(jax.random.fold_in(arg_keys[10], 71), 0)
    lengths = draw_lengths(jax.random.fold_in(arg_keys[10], 71), 0)
    out_weight = gaussian(arg_keys[3], (QH * HD, D), QH ** -0.5, 1.0, ((0, 16),))
    resid = gaussian(arg_keys[4], (ROWS, D), 1.0, 6.0, ((0, 8),))
    norm_gain = jnp.clip(1.0 + 0.18 * jax.random.normal(arg_keys[5], (D,), jnp.float32), 0.1, 1.9)
    expert_ids_keys = jax.random.split(jax.random.fold_in(arg_keys[6], 1), ROWS // ROWS_GRP)
    expert_ids_turns = jax.random.permutation(jax.random.fold_in(arg_keys[6], 3), ROWS // ROWS_GRP)
    expert_ids = jax.vmap(lambda own, number: assign_block(jax.random.fold_in(arg_keys[6], 2), own, number, ROWS_GRP, EXPERTS, TOPK, CAP, 2))(expert_ids_keys, expert_ids_turns).reshape((ROWS, TOPK))
    expert_gates = jnp.clip(jnp.exp(math.log(1.0) - 2.9957323 * jax.random.uniform(arg_keys[7], (ROWS, TOPK), jnp.float32) ** level_of(arg_keys[7], (ROWS, TOPK), ((0, 8),), -0.2, 0.2)), 0.05, 1.0)
    w_gate_up = gaussian(arg_keys[8], (EXPERTS, D, 2 * FFE), D ** -0.5, 0.125, ((0, 128),))
    w_down = gaussian(arg_keys[9], (EXPERTS, FFE, D), FFE ** -0.5, 0.21875, ((0, 128),))
    return {"queries": queries, "kv_cache": kv_cache, "lengths": lengths, "out_weight": out_weight, "resid": resid, "norm_gain": norm_gain, "expert_ids": expert_ids, "expert_gates": expert_gates, "w_gate_up": w_gate_up, "w_down": w_down}


def reference(queries, kv_cache, lengths, out_weight, resid, norm_gain, expert_ids, expert_gates, w_gate_up, w_down):
    row_total = queries.shape[0]
    group_heads = QH // KVH
    kv_whole = kv_cache.reshape(row_total, KVH, KV_PARTS * L_PART, 2 * HD)
    key_rows = kv_whole[..., :HD].astype(jnp.float32)
    value_rows = kv_whole[..., HD:].astype(jnp.float32)
    query_rows = queries.reshape(row_total, KVH, group_heads, HD).astype(jnp.float32)
    scores = jnp.einsum('rhgd,rhpd->rhgp', query_rows, key_rows) / math.sqrt(HD)
    valid_mask = (jnp.arange(KV_PARTS * L_PART, dtype=jnp.int32)[None, :] < lengths[:, None])[:, None, None, :]
    masked = jnp.where(valid_mask, scores, -1e+30)
    row_max = lax.optimization_barrier(jnp.max(masked, axis=-1, keepdims=True))
    weights = jnp.where(valid_mask, jnp.exp(masked - row_max), 0.0)
    weight_sum = lax.optimization_barrier(jnp.sum(weights, axis=-1))
    probs = lax.optimization_barrier(weights.astype(jnp.bfloat16))
    numerator = jnp.einsum('rhgp,rhpd->rhgd', probs.astype(jnp.float32), value_rows)
    heads_out = (numerator / weight_sum[..., None]).astype(jnp.bfloat16).reshape(row_total, QH * HD)
    projected = jnp.dot(heads_out, out_weight, preferred_element_type=jnp.float32)
    middle = (resid.astype(jnp.float32) + projected).astype(jnp.bfloat16)
    middle_wide = middle.astype(jnp.float32)
    inv_rms = lax.rsqrt(lax.optimization_barrier(jnp.mean(middle_wide * middle_wide, axis=-1, keepdims=True)) + 1e-06)
    normed = (middle_wide * inv_rms * norm_gain).astype(jnp.bfloat16)
    experts = w_gate_up.shape[0]
    matches = expert_ids[:, :, None] == jnp.arange(experts, dtype=jnp.int32)[None, None, :]
    coefficients = lax.optimization_barrier(jnp.sum(jnp.where(matches, expert_gates[:, :, None], 0.0), axis=1))
    routed = jnp.any(matches, axis=1).astype(jnp.int32)
    most_rows = N_GRP * CAP

    def one_expert(accumulated, expert_index):
        flags = jnp.take(routed, expert_index, axis=1)
        row_order = jnp.argsort(1 - flags, stable=True)[:most_rows].astype(jnp.int32)
        picked = normed[row_order]
        hidden = jnp.dot(picked, w_gate_up[expert_index], preferred_element_type=jnp.float32)
        activated = (jax.nn.silu(hidden[:, :FFE]) * hidden[:, FFE:]).astype(jnp.bfloat16)
        result = jnp.dot(activated, w_down[expert_index], preferred_element_type=jnp.float32).astype(jnp.bfloat16)
        weighted = coefficients[row_order, expert_index][:, None] * result.astype(jnp.float32)
        return (accumulated.at[row_order].add(weighted), None)
    moe, _ = lax.scan(one_expert, jnp.zeros((row_total, D), jnp.float32), jnp.arange(experts, dtype=jnp.int32))
    return (middle_wide + moe).astype(jnp.bfloat16)
```

```python
import functools
import math

import jax
import jax.numpy as jnp
from jax import lax
from jax.experimental import pallas as pl
from jax.experimental.pallas import tpu as pltpu
from jax.sharding import PartitionSpec as P

HD = 128
TOPK = 8
NEG = -1e30
F32 = jnp.float32
BF16 = jnp.bfloat16
MESH = pl.DeviceIdType.MESH


def kernel(
    dims,
    len_ref,
    q_hbm,
    kv_hbm,
    ow_hbm,
    resid_hbm,
    gain_ref,
    ids_ref,
    gates_ref,
    wgu_hbm,
    wd_hbm,
    out_ref,
    q_v,
    kv_v,
    ow_v,
    res_v,
    wgu_v,
    wd_v,
    qf,
    num,
    lse,
    a_send,
    a_recv,
    b_send,
    b_recv,
    mid_all,
    d_send,
    d_recv,
    e_send,
    e_recv,
    f_send,
    f_recv,
    kv_sem,
    in_sem,
    send_sem,
    recv_sem,
):
    sides, grps, tps, parts = dims
    members = sides * tps
    rows = q_v.shape[0]
    heads = q_v.shape[1] // HD
    span = kv_v.shape[1]
    width = ow_v.shape[1]
    mine_rows = rows * heads // parts
    inner = wd_v.shape[0]
    side = lax.axis_index("side")
    grp = lax.axis_index("grp")
    tp = lax.axis_index("tp")
    member = side * tps + tp
    part = lax.rem(tp, parts)
    head_group = tp // parts

    def group_peer(d):
        other = lax.rem(member + d, members)
        return other, (other // tps, grp, lax.rem(other, tps))

    def grp_peer(d):
        other = lax.rem(grp + d, grps)
        return other, (side, other, tp)

    def part_peer(d):
        other = lax.rem(part + d, parts)
        return other, (side, grp, head_group * parts + other)

    barrier = pltpu.get_barrier_semaphore()
    for d in range(1, members):
        pl.semaphore_signal(barrier, inc=1, device_id=group_peer(d)[1], device_id_type=MESH)
    for d in range(1, grps):
        pl.semaphore_signal(barrier, inc=1, device_id=grp_peer(d)[1], device_id_type=MESH)

    q_copy = pltpu.make_async_copy(
        q_hbm.at[:, pl.ds(pl.multiple_of(head_group * heads * HD, 128), heads * HD)], q_v, in_sem.at[0]
    )
    q_copy.start()
    kv_copies = []
    chunks = kv_sem.shape[0]
    per_chunk = rows // chunks
    for c in range(chunks):
        copy = pltpu.make_async_copy(
            kv_hbm.at[pl.ds(c * per_chunk, per_chunk), 0], kv_v.at[pl.ds(c * per_chunk, per_chunk)], kv_sem.at[c]
        )
        copy.start()
        kv_copies.append(copy)
    ow_copy = pltpu.make_async_copy(ow_hbm, ow_v, in_sem.at[1])
    ow_copy.start()
    res_copy = pltpu.make_async_copy(
        resid_hbm.at[:, pl.ds(pl.multiple_of(member * 128, 128), 128)], res_v, in_sem.at[2]
    )
    res_copy.start()
    wgu_copy = pltpu.make_async_copy(wgu_hbm.at[0], wgu_v, in_sem.at[3])
    wgu_copy.start()
    wd_copy = pltpu.make_async_copy(wd_hbm.at[0], wd_v, in_sem.at[4])
    wd_copy.start()

    slots = grps * 4
    col = lax.broadcasted_iota(jnp.int32, (rows, slots), 1)
    expert = (side * grps + col // 4) * tps + tp
    ids = ids_ref[...]
    gates = gates_ref[...]
    hit = jnp.zeros((rows, slots), F32)
    gate_cols = jnp.zeros((rows, slots), F32)
    for k in range(TOPK):
        same = ids[:, k : k + 1] == expert
        hit = jnp.where(same, 1.0, hit)
        gate_cols = jnp.where(same, gates[:, k : k + 1], gate_cols)
    below = (
        lax.broadcasted_iota(jnp.int32, (rows, rows), 1) < lax.broadcasted_iota(jnp.int32, (rows, rows), 0)
    ).astype(F32)
    rank = jnp.dot(below.astype(BF16), hit.astype(BF16), preferred_element_type=F32)
    placed = jnp.where(rank == (col % 4).astype(F32), hit, 0.0)
    combine = placed * gate_cols
    combine_hi = combine.astype(BF16)
    combine_lo = (combine - combine_hi.astype(F32)).astype(BF16)

    q_copy.wait()
    for j in range(heads):
        qf[j * rows : (j + 1) * rows, :] = q_v[:, j * HD : (j + 1) * HD].astype(F32)
    first = part * span
    position = first + lax.broadcasted_iota(jnp.int32, (heads, span), 1)
    scale = 1.0 / math.sqrt(HD)
    for c in range(chunks):
        kv_copies[c].wait()
        for r in range(c * per_chunk, (c + 1) * per_chunk):
            query = qf[pl.ds(r, heads, stride=rows), :].astype(BF16)
            scores = lax.dot_general(
                query, kv_v[r, :, :HD], (((1,), (1,)), ((), ())), preferred_element_type=F32
            )
            valid = position < len_ref[r]
            scores = jnp.where(valid, scores * scale, NEG)
            top = jnp.max(scores, axis=1, keepdims=True)
            weights = jnp.where(valid, jnp.exp(scores - top), 0.0)
            total = jnp.sum(weights, axis=1, keepdims=True)
            value = jnp.dot(weights.astype(BF16), kv_v[r, :, HD:], preferred_element_type=F32)
            some = total > 0.0
            safe = jnp.where(some, total, 1.0)
            num[pl.ds(r, heads, stride=rows), :] = value * (1.0 / safe)
            lse[pl.ds(r, heads, stride=rows), :] = jnp.broadcast_to(
                jnp.where(some, top + jnp.log(safe), NEG), (heads, HD)
            )

    diagonal = lax.broadcasted_iota(jnp.int32, (mine_rows, HD), 0) == lax.broadcasted_iota(
        jnp.int32, (mine_rows, HD), 1
    )
    line = lax.broadcasted_iota(jnp.int32, (16, HD), 0)
    for p in range(parts):
        block = slice(p * mine_rows, (p + 1) * mine_rows)
        a_send[p, :mine_rows, :] = num[block, :].astype(BF16)
        stat = jnp.sum(jnp.where(diagonal, lse[block, :], 0.0), axis=0, keepdims=True)
        high = stat.astype(BF16).astype(F32)
        middle_word = (stat - high).astype(BF16).astype(F32)
        low = stat - high - middle_word
        words = jnp.where(line == 0, high, jnp.where(line == 1, middle_word, jnp.where(line == 2, low, 0.0)))
        a_send[p, mine_rows:, :] = words.astype(BF16)

    pl.semaphore_wait(barrier, members + grps - 2)

    def send(src, dst, index, device):
        pltpu.make_async_remote_copy(
            src_ref=src,
            dst_ref=dst,
            send_sem=send_sem.at[index],
            recv_sem=recv_sem.at[index],
            device_id=device,
            device_id_type=MESH,
        ).start()

    def totals(src, dst, index, device):
        return pltpu.make_async_remote_copy(
            src_ref=src,
            dst_ref=dst,
            send_sem=send_sem.at[index],
            recv_sem=recv_sem.at[index],
            device_id=device,
            device_id_type=MESH,
        )

    for d in range(1, parts):
        other, device = part_peer(d)
        send(a_send.at[other], a_recv.at[d - 1], 0, device)
    first_peer = part_peer(1)[1]
    done_a = totals(a_send.at[pl.ds(0, parts - 1)], a_recv, 0, first_peer)
    own = pl.ds(pl.multiple_of(part * mine_rows, 8), mine_rows)
    values = [num[own, :]]
    levels = [lse[own, :][:, 0:1]]
    done_a.wait_recv()
    for d in range(parts - 1):
        values.append(a_recv[d, :mine_rows, :].astype(F32))
        row = jnp.sum(a_recv[d, mine_rows:, :].astype(F32), axis=0, keepdims=True)
        levels.append(jnp.sum(jnp.where(diagonal, row, 0.0), axis=1, keepdims=True))
    peak = functools.reduce(jnp.maximum, levels)
    shares = [jnp.exp(level - peak) for level in levels]
    whole = functools.reduce(jnp.add, shares)
    merged = functools.reduce(jnp.add, [v * s for v, s in zip(values, shares)]) * (1.0 / whole)
    per_member = mine_rows // rows
    attended = jnp.concatenate(
        [merged[i * rows : (i + 1) * rows, :] for i in range(per_member)], axis=1
    ).astype(BF16)

    ow_copy.wait()
    projected = jnp.dot(attended, ow_v[...], preferred_element_type=F32)
    for j in range(members):
        b_send[j, :, :] = projected[:, j * 128 : (j + 1) * 128].astype(BF16)
    for d in range(1, members):
        other, device = group_peer(d)
        send(b_send.at[other], b_recv.at[d - 1], 1, device)
    group_first = group_peer(1)[1]
    done_b = totals(b_send.at[pl.ds(0, members - 1)], b_recv, 1, group_first)
    res_copy.wait()
    acc = res_v[...].astype(F32) + b_send[member, :, :].astype(F32)
    done_b.wait_recv()
    for d in range(members - 1):
        acc = acc + b_recv[d, :, :].astype(F32)
    mine = acc.astype(BF16)
    mid_all[member, :, :] = mine

    for d in range(1, members):
        _, device = group_peer(d)
        send(mid_all.at[member], mid_all.at[member], 2, device)
    done_c = totals(mid_all.at[pl.ds(0, members - 1)], mid_all.at[pl.ds(0, members - 1)], 2, group_first)
    done_c.wait_recv()
    square = jnp.zeros((rows, 128), F32)
    for j in range(members):
        wide = mid_all[j, :, :].astype(F32)
        square = square + wide * wide
    inv_rms = lax.rsqrt(jnp.sum(square, axis=1, keepdims=True) * (1.0 / width) + 1e-6)
    normed = jnp.concatenate(
        [(mid_all[j, :, :].astype(F32) * inv_rms * gain_ref[j : j + 1, :]).astype(BF16) for j in range(members)],
        axis=1,
    )
    chosen = lax.dot_general(
        placed.astype(BF16), normed, (((0,), (0,)), ((), ())), preferred_element_type=F32
    )

    for g in range(grps):
        d_send[g, :, :] = chosen[g * 4 : (g + 1) * 4, :].astype(BF16)
    for d in range(1, grps):
        other, device = grp_peer(d)
        send(d_send.at[other], d_recv.at[grp], 3, device)
    grp_first = grp_peer(1)[1]
    done_d = totals(d_send.at[pl.ds(0, grps - 1)], d_recv.at[pl.ds(0, grps - 1)], 3, grp_first)
    d_recv[grp, :, :] = d_send[grp, :, :]
    wgu_copy.wait()
    done_d.wait_recv()
    arrived = jnp.concatenate([d_recv[g, :, :].astype(F32) for g in range(grps)], axis=0).astype(BF16)
    both = jnp.dot(arrived, wgu_v[...], preferred_element_type=F32)
    gate = both[:, :inner]
    act = (gate / (1.0 + jnp.exp(-gate)) * both[:, inner:]).astype(BF16)
    wd_copy.wait()
    produced = jnp.dot(act, wd_v[...], preferred_element_type=F32)

    for g in range(grps):
        e_send[g, :, :] = produced[g * 4 : (g + 1) * 4, :].astype(BF16)
    for d in range(1, grps):
        other, device = grp_peer(d)
        send(e_send.at[other], e_recv.at[grp], 4, device)
    done_e = totals(e_send.at[pl.ds(0, grps - 1)], e_recv.at[pl.ds(0, grps - 1)], 4, grp_first)
    e_recv[grp, :, :] = e_send[grp, :, :]
    done_e.wait_recv()
    returned = jnp.concatenate([e_recv[g, :, :].astype(F32) for g in range(grps)], axis=0).astype(BF16)
    gated = jnp.dot(combine_hi, returned, preferred_element_type=F32) + jnp.dot(
        combine_lo, returned, preferred_element_type=F32
    )

    for j in range(members):
        f_send[j, :, :] = gated[:, j * 128 : (j + 1) * 128].astype(BF16)
    for d in range(1, members):
        other, device = group_peer(d)
        send(f_send.at[other], f_recv.at[d - 1], 5, device)
    done_f = totals(f_send.at[pl.ds(0, members - 1)], f_recv, 5, group_first)
    final = mid_all[member, :, :].astype(F32) + f_send[member, :, :].astype(F32)
    done_f.wait_recv()
    for d in range(members - 1):
        final = final + f_recv[d, :, :].astype(F32)
    out_ref[...] = final.astype(BF16)
    for done in (done_a, done_b, done_c, done_d, done_e, done_f):
        done.wait_send()


def body(queries, kv_cache, lengths, out_weight, resid, norm_gain, expert_ids, expert_gates, w_gate_up, w_down):
    sides, grps, tps = lax.axis_size("side"), lax.axis_size("grp"), lax.axis_size("tp")
    members = sides * tps
    rows = queries.shape[0]
    parts = 4
    heads = 8
    span = kv_cache.shape[2]
    width = out_weight.shape[1]
    mine_rows = rows * heads // parts
    vmem = pl.BlockSpec(memory_space=pltpu.VMEM)
    anywhere = pl.BlockSpec(memory_space=pl.ANY)
    return pl.pallas_call(
        functools.partial(kernel, (sides, grps, tps, parts)),
        out_shape=jax.ShapeDtypeStruct((rows, width // members), BF16),
        in_specs=[
            pl.BlockSpec(memory_space=pltpu.SMEM),
            anywhere,
            anywhere,
            anywhere,
            anywhere,
            vmem,
            vmem,
            vmem,
            anywhere,
            anywhere,
        ],
        out_specs=vmem,
        scratch_shapes=[
            pltpu.VMEM((rows, heads * HD), BF16),
            pltpu.VMEM((rows, span, 2 * HD), BF16),
            pltpu.VMEM(out_weight.shape, BF16),
            pltpu.VMEM((rows, 128), BF16),
            pltpu.VMEM(w_gate_up.shape[1:], BF16),
            pltpu.VMEM(w_down.shape[1:], BF16),
            pltpu.VMEM((rows * heads, HD), F32),
            pltpu.VMEM((rows * heads, HD), F32),
            pltpu.VMEM((rows * heads, HD), F32),
            pltpu.VMEM((parts, mine_rows + 16, HD), BF16),
            pltpu.VMEM((parts - 1, mine_rows + 16, HD), BF16),
            pltpu.VMEM((members, rows, 128), BF16),
            pltpu.VMEM((members - 1, rows, 128), BF16),
            pltpu.VMEM((members, rows, 128), BF16),
            pltpu.VMEM((grps, 4, width), BF16),
            pltpu.VMEM((grps, 4, width), BF16),
            pltpu.VMEM((grps, 4, width), BF16),
            pltpu.VMEM((grps, 4, width), BF16),
            pltpu.VMEM((members, rows, 128), BF16),
            pltpu.VMEM((members - 1, rows, 128), BF16),
            pltpu.SemaphoreType.DMA((4,)),
            pltpu.SemaphoreType.DMA((5,)),
            pltpu.SemaphoreType.DMA((6,)),
            pltpu.SemaphoreType.DMA((6,)),
        ],
        compiler_params=pltpu.CompilerParams(
            collective_id=0, has_side_effects=True, vmem_limit_bytes=56 * 1024 * 1024
        ),
        name="layer",
    )(
        lengths,
        queries,
        kv_cache,
        out_weight,
        resid,
        norm_gain.reshape(members, width // members),
        expert_ids,
        expert_gates,
        w_gate_up,
        w_down,
    )


def solution(mesh):
    in_specs = (
        P("grp", "side"),
        P("grp", ("side", "tp"), None, None),
        P("grp"),
        P(("side", "tp"), None),
        P("grp", None),
        P(),
        P("grp", None),
        P("grp", None),
        P(("side", "grp", "tp"), None, None),
        P(("side", "grp", "tp"), None, None),
    )
    out_specs = P("grp", ("side", "tp"))
    return jax.shard_map(body, mesh=mesh, in_specs=in_specs, out_specs=out_specs, check_vma=False)
```

```python
import functools
import math

import jax
import jax.numpy as jnp
from jax import lax
from jax.experimental import pallas as pl
from jax.experimental.pallas import tpu as pltpu
from jax.sharding import PartitionSpec as P

HD = 128
TOPK = 8
SLOTS = 4
NEG = -1e30
F32 = jnp.float32
BF16 = jnp.bfloat16
MESH = pl.DeviceIdType.MESH


def kernel(
    dims,
    len_hbm,
    q_hbm,
    kv_hbm,
    ow_hbm,
    resid_hbm,
    gain_hbm,
    ids_hbm,
    gates_hbm,
    wgu_hbm,
    wd_hbm,
    out_ref,
    len_ref,
    gain_v,
    ids_v,
    gates_v,
    q_v,
    kv_v,
    ow_v,
    res_v,
    wgu_v,
    wd_v,
    qf,
    num,
    lse,
    pick,
    mix,
    a_send,
    a_recv,
    b_send,
    b_recv,
    d_send,
    d_recv,
    e_send,
    e_recv,
    small_sem,
    kv_sem,
    in_sem,
    send_sem,
    recv_sem,
):
    sides, grps, tps, parts = dims
    members = sides * tps
    experts = members * grps
    rows = q_v.shape[0]
    heads = q_v.shape[1] // HD
    span = kv_v.shape[1]
    width = ow_v.shape[1]
    mine_rows = rows * heads // parts
    inner = wd_v.shape[0]
    side = lax.axis_index("side")
    grp = lax.axis_index("grp")
    tp = lax.axis_index("tp")
    member = side * tps + tp
    part = lax.rem(tp, parts)
    head_group = tp // parts
    groups = tps // parts
    mine_expert = (side * grps + grp) * tps + tp

    grp_low = 4 if grps % 4 == 0 else grps
    grp_high = grps // grp_low
    side_at = [lax.rem(side + d, sides) for d in range(sides)]
    grp_at = {}
    for hi in range(grp_high):
        for lo in range(grp_low):
            grp_at[hi, lo] = lax.rem(grp // grp_low + hi, grp_high) * grp_low + lax.rem(
                lax.rem(grp, grp_low) + lo, grp_low
            )
    tp_at = {}
    for hi in range(groups):
        for lo in range(parts):
            tp_at[hi, lo] = lax.rem(head_group + hi, groups) * parts + lax.rem(part + lo, parts)

    def ring(d, size):
        return min(d, size - d)

    offsets = []
    for ds in range(sides):
        for gh, gl in grp_at:
            for th, tl in tp_at:
                if ds or gh or gl or th or tl:
                    far = 2 * gh + ring(gl, grp_low) + th + ring(tl, parts)
                    offsets.append((-far, ds, gh, gl, th, tl))
    offsets.sort()
    everyone = [(side_at[ds], grp_at[gh, gl], tp_at[th, tl]) for _, ds, gh, gl, th, tl in offsets]
    row_group = [
        (side_at[ds], grp, tp_at[th, tl]) for _, ds, gh, gl, th, tl in offsets if not (gh or gl)
    ]
    column = [(side, grp_at[gh, gl], tp) for _, ds, gh, gl, th, tl in offsets if not (ds or th or tl)]
    same_head = [
        (side, grp, tp_at[th, tl]) for _, ds, gh, gl, th, tl in offsets if not (ds or gh or gl or th)
    ]

    q_copy = pltpu.make_async_copy(
        q_hbm.at[:, pl.ds(pl.multiple_of(head_group * heads * HD, 128), heads * HD)], q_v, in_sem.at[0]
    )
    q_copy.start()
    len_copy = pltpu.make_async_copy(len_hbm, len_ref, small_sem.at[0])
    len_copy.start()
    kv_copies = []
    chunks = kv_sem.shape[0]
    per_chunk = rows // chunks
    for c in range(chunks):
        copy = pltpu.make_async_copy(
            kv_hbm.at[pl.ds(c * per_chunk, per_chunk), 0], kv_v.at[pl.ds(c * per_chunk, per_chunk)], kv_sem.at[c]
        )
        copy.start()
        kv_copies.append(copy)

    barrier = pltpu.get_barrier_semaphore()
    for device in column + row_group:
        pl.semaphore_signal(barrier, inc=1, device_id=device, device_id_type=MESH)

    ids_copy = pltpu.make_async_copy(ids_hbm, ids_v, small_sem.at[1])
    ids_copy.start()
    gates_copy = pltpu.make_async_copy(gates_hbm, gates_v, small_sem.at[2])
    gates_copy.start()
    gain_copy = pltpu.make_async_copy(gain_hbm, gain_v, small_sem.at[3])
    gain_copy.start()
    ow_copy = pltpu.make_async_copy(ow_hbm, ow_v, in_sem.at[1])
    ow_copy.start()
    res_copy = pltpu.make_async_copy(
        resid_hbm.at[:, pl.ds(pl.multiple_of(member * 128, 128), 128)], res_v, in_sem.at[2]
    )
    res_copy.start()
    wgu_copy = pltpu.make_async_copy(wgu_hbm.at[0], wgu_v, in_sem.at[3])
    wgu_copy.start()
    wd_copy = pltpu.make_async_copy(wd_hbm.at[0], wd_v, in_sem.at[4])
    wd_copy.start()

    ids_copy.wait()
    gates_copy.wait()
    eye = (
        lax.broadcasted_iota(jnp.int32, (TOPK, TOPK), 0) == lax.broadcasted_iota(jnp.int32, (TOPK, TOPK), 1)
    ).astype(BF16)

    def flipped(value):
        return lax.dot_general(value.astype(BF16), eye, (((0,), (0,)), ((), ())), preferred_element_type=F32)

    gates_t = gates_v[...]
    gates_high = gates_t.astype(BF16).astype(F32)
    gates_middle = (gates_t - gates_high).astype(BF16).astype(F32)
    ids = flipped(ids_v[...].astype(F32))
    gates = flipped(gates_high) + (flipped(gates_middle) + flipped(gates_t - gates_high - gates_middle))
    col = lax.broadcasted_iota(jnp.int32, (rows, experts * SLOTS), 1)
    expert = (col // SLOTS).astype(F32)
    hit = jnp.zeros((rows, experts * SLOTS), F32)
    gate_cols = jnp.zeros((rows, experts * SLOTS), F32)
    for k in range(TOPK):
        same = ids[:, k : k + 1] == expert
        hit = jnp.where(same, 1.0, hit)
        gate_cols = jnp.where(same, gates[:, k : k + 1], gate_cols)
    below = (
        lax.broadcasted_iota(jnp.int32, (rows, rows), 1) < lax.broadcasted_iota(jnp.int32, (rows, rows), 0)
    ).astype(BF16)
    rank = jnp.dot(below, hit.astype(BF16), preferred_element_type=F32)
    placed = jnp.where(rank == (col % SLOTS).astype(F32), hit, 0.0)
    same_row = (
        lax.broadcasted_iota(jnp.int32, (rows, rows), 1) == lax.broadcasted_iota(jnp.int32, (rows, rows), 0)
    ).astype(BF16)
    pick[...] = lax.dot_general(
        placed.astype(BF16), same_row, (((0,), (0,)), ((), ())), preferred_element_type=F32
    ).astype(BF16)
    combine = placed * gate_cols
    combine_high = combine.astype(BF16).astype(F32)
    mix[...] = jnp.concatenate([combine_high, combine - combine_high], axis=0).astype(BF16)

    q_copy.wait()
    for j in range(heads):
        qf[j * rows : (j + 1) * rows, :] = q_v[:, j * HD : (j + 1) * HD].astype(F32)
    len_copy.wait()
    first = part * span
    position = first + lax.broadcasted_iota(jnp.int32, (heads, span), 1)
    scale = 1.0 / math.sqrt(HD)
    for c in range(chunks):
        kv_copies[c].wait()
        for r in range(c * per_chunk, (c + 1) * per_chunk):
            query = qf[pl.ds(r, heads, stride=rows), :].astype(BF16)
            scores = lax.dot_general(
                query, kv_v[r, :, :HD], (((1,), (1,)), ((), ())), preferred_element_type=F32
            )
            valid = position < len_ref[r]
            scores = jnp.where(valid, scores * scale, NEG)
            top = jnp.max(scores, axis=1, keepdims=True)
            weights = jnp.where(valid, jnp.exp(scores - top), 0.0)
            total = jnp.sum(weights, axis=1, keepdims=True)
            value = jnp.dot(weights.astype(BF16), kv_v[r, :, HD:], preferred_element_type=F32)
            some = total > 0.0
            safe = jnp.where(some, total, 1.0)
            num[pl.ds(r, heads, stride=rows), :] = value * (1.0 / safe)
            lse[pl.ds(r, heads, stride=rows), :] = jnp.broadcast_to(
                jnp.where(some, top + jnp.log(safe), NEG), (heads, HD)
            )

    diagonal = lax.broadcasted_iota(jnp.int32, (mine_rows, HD), 0) == lax.broadcasted_iota(
        jnp.int32, (mine_rows, HD), 1
    )
    line = lax.broadcasted_iota(jnp.int32, (16, HD), 0)
    for p in range(parts):
        block = slice(p * mine_rows, (p + 1) * mine_rows)
        a_send[p, :mine_rows, :] = num[block, :].astype(BF16)
        stat = jnp.sum(jnp.where(diagonal, lse[block, :], 0.0), axis=0, keepdims=True)
        high = stat.astype(BF16).astype(F32)
        middle_word = (stat - high).astype(BF16).astype(F32)
        low = stat - high - middle_word
        words = jnp.where(line == 0, high, jnp.where(line == 1, middle_word, jnp.where(line == 2, low, 0.0)))
        a_send[p, mine_rows:, :] = words.astype(BF16)

    pl.semaphore_wait(barrier, members + grps - 2)

    def remote(src, dst, index, device):
        return pltpu.make_async_remote_copy(
            src_ref=src,
            dst_ref=dst,
            send_sem=send_sem.at[index],
            recv_sem=recv_sem.at[index],
            device_id=device,
            device_id_type=MESH,
        )

    for i, device in enumerate(same_head):
        remote(a_send.at[lax.rem(device[2], parts)], a_recv.at[i], 0, device).start()
    done_a = remote(a_send.at[pl.ds(0, parts - 1)], a_recv, 0, same_head[0])
    own = pl.ds(pl.multiple_of(part * mine_rows, 8), mine_rows)
    values = [num[own, :]]
    levels = [lse[own, :][:, 0:1]]
    done_a.wait_recv()
    for d in range(parts - 1):
        values.append(a_recv[d, :mine_rows, :].astype(F32))
        row = jnp.sum(a_recv[d, mine_rows:, :].astype(F32), axis=0, keepdims=True)
        levels.append(jnp.sum(jnp.where(diagonal, row, 0.0), axis=1, keepdims=True))
    peak = functools.reduce(jnp.maximum, levels)
    shares = [jnp.exp(level - peak) for level in levels]
    whole = functools.reduce(jnp.add, shares)
    merged = functools.reduce(jnp.add, [v * s for v, s in zip(values, shares)]) * (1.0 / whole)
    per_member = mine_rows // rows
    attended = jnp.concatenate(
        [merged[i * rows : (i + 1) * rows, :] for i in range(per_member)], axis=1
    ).astype(BF16)

    ow_copy.wait()
    projected = jnp.dot(attended, ow_v[...], preferred_element_type=F32)
    for j in range(members):
        b_send[j, :, :] = projected[:, j * 128 : (j + 1) * 128].astype(BF16)
    for i, device in enumerate(row_group):
        remote(b_send.at[device[0] * tps + device[2]], b_recv.at[i], 1, device).start()
    done_b = remote(b_send.at[pl.ds(0, members - 1)], b_recv, 1, row_group[0])
    res_copy.wait()
    acc = res_v[...].astype(F32) + b_send[member, :, :].astype(F32)
    done_b.wait_recv()
    for d in range(members - 1):
        acc = acc + b_recv[d, :, :].astype(F32)
    middle = acc.astype(BF16)

    chosen = jnp.dot(pick[...], middle, preferred_element_type=F32).astype(BF16)
    d_send[...] = chosen.reshape(experts, SLOTS, 128)
    slot = member * grps + grp
    for device in everyone:
        remote(d_send.at[(device[0] * grps + device[1]) * tps + device[2]], d_recv.at[slot], 2, device).start()
    d_recv[slot, :, :] = d_send[mine_expert, :, :]
    done_d = remote(d_send.at[pl.ds(0, experts - 1)], d_recv.at[pl.ds(0, experts - 1)], 2, everyone[0])
    gain_copy.wait()
    wgu_copy.wait()
    done_d.wait_recv()
    pieces = [
        d_recv[j * grps : (j + 1) * grps, :, :].reshape(grps * SLOTS, 128).astype(F32) for j in range(members)
    ]
    square = functools.reduce(jnp.add, [piece * piece for piece in pieces])
    inv_rms = lax.rsqrt(jnp.sum(square, axis=1, keepdims=True) * (1.0 / width) + 1e-6)
    normed = jnp.concatenate(
        [(piece * inv_rms * gain_v[j : j + 1, :]).astype(BF16) for j, piece in enumerate(pieces)], axis=1
    )
    both = jnp.dot(normed, wgu_v[...], preferred_element_type=F32)
    gate = both[:, :inner]
    act = (gate / (1.0 + jnp.exp(-gate)) * both[:, inner:]).astype(BF16)
    wd_copy.wait()
    produced = jnp.dot(act, wd_v[...], preferred_element_type=F32).astype(BF16)

    for j in range(members):
        e_send[:, j, :, :] = produced[:, j * 128 : (j + 1) * 128].reshape(grps, SLOTS, 128)
    for device in everyone:
        remote(e_send.at[device[1], device[0] * tps + device[2]], e_recv.at[mine_expert], 3, device).start()
    e_recv[mine_expert, :, :] = e_send[grp, member, :, :]
    done_e = remote(e_recv.at[pl.ds(0, experts - 1)], e_recv.at[pl.ds(0, experts - 1)], 3, everyone[0])
    done_e.wait_recv()
    returned = e_recv[...].reshape(experts * SLOTS, 128)
    gated = jnp.dot(mix[...], returned, preferred_element_type=F32)
    out_ref[...] = (middle.astype(F32) + (gated[:rows, :] + gated[rows:, :])).astype(BF16)
    for done in (done_a, done_b, done_d, done_e):
        done.wait_send()


def body(queries, kv_cache, lengths, out_weight, resid, norm_gain, expert_ids, expert_gates, w_gate_up, w_down):
    sides, grps, tps = lax.axis_size("side"), lax.axis_size("grp"), lax.axis_size("tp")
    members = sides * tps
    experts = members * grps
    rows = queries.shape[0]
    parts = 4
    heads = 8
    span = kv_cache.shape[2]
    width = out_weight.shape[1]
    mine_rows = rows * heads // parts
    anywhere = pl.BlockSpec(memory_space=pl.ANY)
    return pl.pallas_call(
        functools.partial(kernel, (sides, grps, tps, parts)),
        out_shape=jax.ShapeDtypeStruct((rows, width // members), BF16),
        in_specs=[anywhere] * 10,
        out_specs=pl.BlockSpec(memory_space=pltpu.VMEM),
        scratch_shapes=[
            pltpu.SMEM((rows,), jnp.int32),
            pltpu.VMEM((members, width // members), F32),
            pltpu.VMEM((TOPK, rows), jnp.int32),
            pltpu.VMEM((TOPK, rows), F32),
            pltpu.VMEM((rows, heads * HD), BF16),
            pltpu.VMEM((rows, span, 2 * HD), BF16),
            pltpu.VMEM(out_weight.shape, BF16),
            pltpu.VMEM((rows, 128), BF16),
            pltpu.VMEM(w_gate_up.shape[1:], BF16),
            pltpu.VMEM(w_down.shape[1:], BF16),
            pltpu.VMEM((rows * heads, HD), F32),
            pltpu.VMEM((rows * heads, HD), F32),
            pltpu.VMEM((rows * heads, HD), F32),
            pltpu.VMEM((experts * SLOTS, rows), BF16),
            pltpu.VMEM((2 * rows, experts * SLOTS), BF16),
            pltpu.VMEM((parts, mine_rows + 16, HD), BF16),
            pltpu.VMEM((parts - 1, mine_rows + 16, HD), BF16),
            pltpu.VMEM((members, rows, 128), BF16),
            pltpu.VMEM((members - 1, rows, 128), BF16),
            pltpu.VMEM((experts, SLOTS, 128), BF16),
            pltpu.VMEM((experts, SLOTS, 128), BF16),
            pltpu.VMEM((grps, members, SLOTS, 128), BF16),
            pltpu.VMEM((experts, SLOTS, 128), BF16),
            pltpu.SemaphoreType.DMA((4,)),
            pltpu.SemaphoreType.DMA((4,)),
            pltpu.SemaphoreType.DMA((5,)),
            pltpu.SemaphoreType.DMA((4,)),
            pltpu.SemaphoreType.DMA((4,)),
        ],
        compiler_params=pltpu.CompilerParams(
            collective_id=0, has_side_effects=True, vmem_limit_bytes=56 * 1024 * 1024
        ),
        name="layer",
    )(
        lengths,
        queries,
        kv_cache,
        out_weight,
        resid,
        norm_gain.reshape(members, width // members),
        expert_ids.T,
        expert_gates.T,
        w_gate_up,
        w_down,
    )


def solution(mesh):
    in_specs = (
        P("grp", "side"),
        P("grp", ("side", "tp"), None, None),
        P("grp"),
        P(("side", "tp"), None),
        P("grp", None),
        P(),
        P("grp", None),
        P("grp", None),
        P(("side", "grp", "tp"), None, None),
        P(("side", "grp", "tp"), None, None),
    )
    out_specs = P("grp", ("side", "tp"))
    return jax.shard_map(body, mesh=mesh, in_specs=in_specs, out_specs=out_specs, check_vma=False)
```

```python
import functools
import math

import jax
import jax.numpy as jnp
from jax import lax
from jax.experimental import pallas as pl
from jax.experimental.pallas import tpu as pltpu
from jax.sharding import PartitionSpec as P

HD = 128
TOPK = 8
SLOTS = 4
NEG = -1e30
F32 = jnp.float32
BF16 = jnp.bfloat16
MESH = pl.DeviceIdType.MESH


def kernel(
    dims,
    len_hbm,
    q_hbm,
    kv_hbm,
    ow_hbm,
    resid_hbm,
    gain_hbm,
    ids_hbm,
    gates_hbm,
    wgu_hbm,
    wd_hbm,
    out_ref,
    len_ref,
    gain_v,
    ids_v,
    gates_v,
    q_v,
    kv_v,
    ow_v,
    res_v,
    wgu_v,
    wd_v,
    qf,
    num,
    lse,
    pick,
    mix,
    a_send,
    a_recv,
    b_send,
    b_recv,
    d_send,
    d_recv,
    e_send,
    e_recv,
    small_sem,
    kv_sem,
    in_sem,
    send_sem,
    recv_sem,
):
    sides, grps, tps, parts = dims
    members = sides * tps
    experts = members * grps
    rows = q_v.shape[0]
    heads = q_v.shape[1] // HD
    span = kv_v.shape[1]
    width = ow_v.shape[1]
    mine_rows = rows * heads // parts
    inner = wd_v.shape[0]
    side = lax.axis_index("side")
    grp = lax.axis_index("grp")
    tp = lax.axis_index("tp")
    member = side * tps + tp
    part = lax.rem(tp, parts)
    head_group = tp // parts
    groups = tps // parts
    mine_expert = (side * grps + grp) * tps + tp

    grp_low = 4 if grps % 4 == 0 else grps
    grp_high = grps // grp_low
    side_at = [lax.rem(side + d, sides) for d in range(sides)]
    grp_at = {}
    for hi in range(grp_high):
        for lo in range(grp_low):
            grp_at[hi, lo] = lax.rem(grp // grp_low + hi, grp_high) * grp_low + lax.rem(
                lax.rem(grp, grp_low) + lo, grp_low
            )
    tp_at = {}
    for hi in range(groups):
        for lo in range(parts):
            tp_at[hi, lo] = lax.rem(head_group + hi, groups) * parts + lax.rem(part + lo, parts)

    def ring(d, size):
        return min(d, size - d)

    offsets = []
    for ds in range(sides):
        for gh, gl in grp_at:
            for th, tl in tp_at:
                if ds or gh or gl or th or tl:
                    far = 2 * gh + ring(gl, grp_low) + th + ring(tl, parts)
                    offsets.append((-far, ds, gh, gl, th, tl))
    offsets.sort()
    everyone = [(side_at[ds], grp_at[gh, gl], tp_at[th, tl]) for _, ds, gh, gl, th, tl in offsets]
    row_group = [
        (side_at[ds], grp, tp_at[th, tl]) for _, ds, gh, gl, th, tl in offsets if not (gh or gl)
    ]
    column = [(side, grp_at[gh, gl], tp) for _, ds, gh, gl, th, tl in offsets if not (ds or th or tl)]
    same_head = [
        (side, grp, tp_at[th, tl]) for _, ds, gh, gl, th, tl in offsets if not (ds or gh or gl or th)
    ]

    q_copy = pltpu.make_async_copy(
        q_hbm.at[:, pl.ds(pl.multiple_of(head_group * heads * HD, 128), heads * HD)], q_v, in_sem.at[0]
    )
    q_copy.start()
    len_copy = pltpu.make_async_copy(len_hbm, len_ref, small_sem.at[0])
    len_copy.start()
    kv_copies = []
    chunks = kv_sem.shape[0]
    per_chunk = rows // chunks
    for c in range(chunks):
        copy = pltpu.make_async_copy(
            kv_hbm.at[pl.ds(c * per_chunk, per_chunk), 0], kv_v.at[pl.ds(c * per_chunk, per_chunk)], kv_sem.at[c]
        )
        copy.start()
        kv_copies.append(copy)

    barrier = pltpu.get_barrier_semaphore()
    for device in column + row_group:
        pl.semaphore_signal(barrier, inc=1, device_id=device, device_id_type=MESH)

    ids_copy = pltpu.make_async_copy(ids_hbm, ids_v, small_sem.at[1])
    ids_copy.start()
    gates_copy = pltpu.make_async_copy(gates_hbm, gates_v, small_sem.at[2])
    gates_copy.start()
    gain_copy = pltpu.make_async_copy(gain_hbm, gain_v, small_sem.at[3])
    gain_copy.start()
    ow_copy = pltpu.make_async_copy(ow_hbm, ow_v, in_sem.at[1])
    ow_copy.start()
    res_copy = pltpu.make_async_copy(
        resid_hbm.at[:, pl.ds(pl.multiple_of(member * 128, 128), 128)], res_v, in_sem.at[2]
    )
    res_copy.start()
    wgu_copy = pltpu.make_async_copy(wgu_hbm.at[0], wgu_v, in_sem.at[3])
    wgu_copy.start()
    wd_copy = pltpu.make_async_copy(wd_hbm.at[0], wd_v, in_sem.at[4])
    wd_copy.start()

    ids_copy.wait()
    gates_copy.wait()
    eye = (
        lax.broadcasted_iota(jnp.int32, (TOPK, TOPK), 0) == lax.broadcasted_iota(jnp.int32, (TOPK, TOPK), 1)
    ).astype(BF16)

    def flipped(value):
        return lax.dot_general(value.astype(BF16), eye, (((0,), (0,)), ((), ())), preferred_element_type=F32)

    gates_t = gates_v[...]
    gates_high = gates_t.astype(BF16).astype(F32)
    gates_middle = (gates_t - gates_high).astype(BF16).astype(F32)
    ids = flipped(ids_v[...].astype(F32))
    gates = flipped(gates_high) + (flipped(gates_middle) + flipped(gates_t - gates_high - gates_middle))
    col = lax.broadcasted_iota(jnp.int32, (rows, experts * SLOTS), 1)
    expert = (col // SLOTS).astype(F32)
    hit = jnp.zeros((rows, experts * SLOTS), F32)
    gate_cols = jnp.zeros((rows, experts * SLOTS), F32)
    for k in range(TOPK):
        same = ids[:, k : k + 1] == expert
        hit = jnp.where(same, 1.0, hit)
        gate_cols = jnp.where(same, gates[:, k : k + 1], gate_cols)
    below = (
        lax.broadcasted_iota(jnp.int32, (rows, rows), 1) < lax.broadcasted_iota(jnp.int32, (rows, rows), 0)
    ).astype(BF16)
    rank = jnp.dot(below, hit.astype(BF16), preferred_element_type=F32)
    placed = jnp.where(rank == (col % SLOTS).astype(F32), hit, 0.0)
    same_row = (
        lax.broadcasted_iota(jnp.int32, (rows, rows), 1) == lax.broadcasted_iota(jnp.int32, (rows, rows), 0)
    ).astype(BF16)
    pick[...] = lax.dot_general(
        placed.astype(BF16), same_row, (((0,), (0,)), ((), ())), preferred_element_type=F32
    ).astype(BF16)
    combine = placed * gate_cols
    combine_high = combine.astype(BF16).astype(F32)
    mix[...] = jnp.concatenate([combine_high, combine - combine_high], axis=0).astype(BF16)

    q_copy.wait()
    for j in range(heads):
        qf[j * rows : (j + 1) * rows, :] = q_v[:, j * HD : (j + 1) * HD].astype(F32)
    len_copy.wait()
    first = part * span
    position = first + lax.broadcasted_iota(jnp.int32, (heads, span), 1)
    scale = 1.0 / math.sqrt(HD)

    def attend_scores(batch):
        made = []
        for r in batch:
            query = qf[pl.ds(r, heads, stride=rows), :].astype(BF16)
            made.append(
                lax.dot_general(query, kv_v[r, :, :HD], (((1,), (1,)), ((), ())), preferred_element_type=F32)
            )
        return made

    def attend_values(batch, made):
        valids = [position < len_ref[r] for r in batch]
        made = [jnp.where(valid, score * scale, NEG) for valid, score in zip(valids, made)]
        tops = [jnp.max(score, axis=1, keepdims=True) for score in made]
        weights = [
            jnp.where(valid, jnp.exp(score - top), 0.0) for valid, score, top in zip(valids, made, tops)
        ]
        totals = [jnp.sum(weight, axis=1, keepdims=True) for weight in weights]
        results = [
            jnp.dot(weight.astype(BF16), kv_v[r, :, HD:], preferred_element_type=F32)
            for r, weight in zip(batch, weights)
        ]
        for r, top, total, value in zip(batch, tops, totals, results):
            some = total > 0.0
            safe = jnp.where(some, total, 1.0)
            num[pl.ds(r, heads, stride=rows), :] = value * (1.0 / safe)
            lse[pl.ds(r, heads, stride=rows), :] = jnp.broadcast_to(
                jnp.where(some, top + jnp.log(safe), NEG), (heads, HD)
            )

    batches = [range(c * per_chunk, (c + 1) * per_chunk) for c in range(chunks)]
    ready = None
    for c in range(chunks):
        kv_copies[c].wait()
        made = attend_scores(batches[c])
        if ready is not None:
            attend_values(batches[c - 1], ready)
        ready = made
    attend_values(batches[-1], ready)

    diagonal = lax.broadcasted_iota(jnp.int32, (mine_rows, HD), 0) == lax.broadcasted_iota(
        jnp.int32, (mine_rows, HD), 1
    )
    line = lax.broadcasted_iota(jnp.int32, (16, HD), 0)
    for p in range(parts):
        block = slice(p * mine_rows, (p + 1) * mine_rows)
        a_send[p, :mine_rows, :] = num[block, :].astype(BF16)
        stat = jnp.sum(jnp.where(diagonal, lse[block, :], 0.0), axis=0, keepdims=True)
        high = stat.astype(BF16).astype(F32)
        middle_word = (stat - high).astype(BF16).astype(F32)
        low = stat - high - middle_word
        words = jnp.where(line == 0, high, jnp.where(line == 1, middle_word, jnp.where(line == 2, low, 0.0)))
        a_send[p, mine_rows:, :] = words.astype(BF16)

    pl.semaphore_wait(barrier, members + grps - 2)

    def remote(src, dst, index, device):
        return pltpu.make_async_remote_copy(
            src_ref=src,
            dst_ref=dst,
            send_sem=send_sem.at[index],
            recv_sem=recv_sem.at[index],
            device_id=device,
            device_id_type=MESH,
        )

    for i, device in enumerate(same_head):
        remote(a_send.at[lax.rem(device[2], parts)], a_recv.at[i], 0, device).start()
    done_a = remote(a_send.at[pl.ds(0, parts - 1)], a_recv, 0, same_head[0])
    own = pl.ds(pl.multiple_of(part * mine_rows, 8), mine_rows)
    values = [num[own, :]]
    levels = [lse[own, :][:, 0:1]]
    done_a.wait_recv()
    for d in range(parts - 1):
        values.append(a_recv[d, :mine_rows, :].astype(F32))
        row = jnp.sum(a_recv[d, mine_rows:, :].astype(F32), axis=0, keepdims=True)
        levels.append(jnp.sum(jnp.where(diagonal, row, 0.0), axis=1, keepdims=True))
    peak = functools.reduce(jnp.maximum, levels)
    shares = [jnp.exp(level - peak) for level in levels]
    whole = functools.reduce(jnp.add, shares)
    merged = functools.reduce(jnp.add, [v * s for v, s in zip(values, shares)]) * (1.0 / whole)
    per_member = mine_rows // rows
    attended = jnp.concatenate(
        [merged[i * rows : (i + 1) * rows, :] for i in range(per_member)], axis=1
    ).astype(BF16)

    ow_copy.wait()
    projected = jnp.dot(attended, ow_v[...], preferred_element_type=F32)
    for j in range(members):
        b_send[j, :, :] = projected[:, j * 128 : (j + 1) * 128].astype(BF16)
    for i, device in enumerate(row_group):
        remote(b_send.at[device[0] * tps + device[2]], b_recv.at[i], 1, device).start()
    done_b = remote(b_send.at[pl.ds(0, members - 1)], b_recv, 1, row_group[0])
    res_copy.wait()
    acc = res_v[...].astype(F32) + b_send[member, :, :].astype(F32)
    done_b.wait_recv()
    for d in range(members - 1):
        acc = acc + b_recv[d, :, :].astype(F32)
    middle = acc.astype(BF16)

    chosen = jnp.dot(pick[...], middle, preferred_element_type=F32).astype(BF16)
    d_send[...] = chosen.reshape(experts, SLOTS, 128)
    slot = member * grps + grp
    for device in everyone:
        remote(d_send.at[(device[0] * grps + device[1]) * tps + device[2]], d_recv.at[slot], 2, device).start()
    d_recv[slot, :, :] = d_send[mine_expert, :, :]
    done_d = remote(d_send.at[pl.ds(0, experts - 1)], d_recv.at[pl.ds(0, experts - 1)], 2, everyone[0])
    gain_copy.wait()
    wgu_copy.wait()
    done_d.wait_recv()
    pieces = [
        d_recv[j * grps : (j + 1) * grps, :, :].reshape(grps * SLOTS, 128).astype(F32) for j in range(members)
    ]
    square = functools.reduce(jnp.add, [piece * piece for piece in pieces])
    inv_rms = lax.rsqrt(jnp.sum(square, axis=1, keepdims=True) * (1.0 / width) + 1e-6)
    normed = jnp.concatenate(
        [(piece * inv_rms * gain_v[j : j + 1, :]).astype(BF16) for j, piece in enumerate(pieces)], axis=1
    )
    both = jnp.dot(normed, wgu_v[...], preferred_element_type=F32)
    gate = both[:, :inner]
    act = (gate / (1.0 + jnp.exp(-gate)) * both[:, inner:]).astype(BF16)
    wd_copy.wait()
    produced = jnp.dot(act, wd_v[...], preferred_element_type=F32).astype(BF16)

    for j in range(members):
        e_send[:, j, :, :] = produced[:, j * 128 : (j + 1) * 128].reshape(grps, SLOTS, 128)
    for device in everyone:
        remote(e_send.at[device[1], device[0] * tps + device[2]], e_recv.at[mine_expert], 3, device).start()
    e_recv[mine_expert, :, :] = e_send[grp, member, :, :]
    done_e = remote(e_recv.at[pl.ds(0, experts - 1)], e_recv.at[pl.ds(0, experts - 1)], 3, everyone[0])
    done_e.wait_recv()
    returned = e_recv[...].reshape(experts * SLOTS, 128)
    gated = jnp.dot(mix[...], returned, preferred_element_type=F32)
    out_ref[...] = (middle.astype(F32) + (gated[:rows, :] + gated[rows:, :])).astype(BF16)
    for done in (done_a, done_b, done_d, done_e):
        done.wait_send()


def body(queries, kv_cache, lengths, out_weight, resid, norm_gain, expert_ids, expert_gates, w_gate_up, w_down):
    sides, grps, tps = lax.axis_size("side"), lax.axis_size("grp"), lax.axis_size("tp")
    members = sides * tps
    experts = members * grps
    rows = queries.shape[0]
    parts = 4
    heads = 8
    span = kv_cache.shape[2]
    width = out_weight.shape[1]
    mine_rows = rows * heads // parts
    anywhere = pl.BlockSpec(memory_space=pl.ANY)
    return pl.pallas_call(
        functools.partial(kernel, (sides, grps, tps, parts)),
        out_shape=jax.ShapeDtypeStruct((rows, width // members), BF16),
        in_specs=[anywhere] * 10,
        out_specs=pl.BlockSpec(memory_space=pltpu.VMEM),
        scratch_shapes=[
            pltpu.SMEM((rows,), jnp.int32),
            pltpu.VMEM((members, width // members), F32),
            pltpu.VMEM((TOPK, rows), jnp.int32),
            pltpu.VMEM((TOPK, rows), F32),
            pltpu.VMEM((rows, heads * HD), BF16),
            pltpu.VMEM((rows, span, 2 * HD), BF16),
            pltpu.VMEM(out_weight.shape, BF16),
            pltpu.VMEM((rows, 128), BF16),
            pltpu.VMEM(w_gate_up.shape[1:], BF16),
            pltpu.VMEM(w_down.shape[1:], BF16),
            pltpu.VMEM((rows * heads, HD), F32),
            pltpu.VMEM((rows * heads, HD), F32),
            pltpu.VMEM((rows * heads, HD), F32),
            pltpu.VMEM((experts * SLOTS, rows), BF16),
            pltpu.VMEM((2 * rows, experts * SLOTS), BF16),
            pltpu.VMEM((parts, mine_rows + 16, HD), BF16),
            pltpu.VMEM((parts - 1, mine_rows + 16, HD), BF16),
            pltpu.VMEM((members, rows, 128), BF16),
            pltpu.VMEM((members - 1, rows, 128), BF16),
            pltpu.VMEM((experts, SLOTS, 128), BF16),
            pltpu.VMEM((experts, SLOTS, 128), BF16),
            pltpu.VMEM((grps, members, SLOTS, 128), BF16),
            pltpu.VMEM((experts, SLOTS, 128), BF16),
            pltpu.SemaphoreType.DMA((4,)),
            pltpu.SemaphoreType.DMA((2,)),
            pltpu.SemaphoreType.DMA((5,)),
            pltpu.SemaphoreType.DMA((4,)),
            pltpu.SemaphoreType.DMA((4,)),
        ],
        compiler_params=pltpu.CompilerParams(
            collective_id=0, has_side_effects=True, vmem_limit_bytes=56 * 1024 * 1024
        ),
        name="layer",
    )(
        lengths,
        queries,
        kv_cache,
        out_weight,
        resid,
        norm_gain.reshape(members, width // members),
        expert_ids.T,
        expert_gates.T,
        w_gate_up,
        w_down,
    )


def solution(mesh):
    in_specs = (
        P("grp", "side"),
        P("grp", ("side", "tp"), None, None),
        P("grp"),
        P(("side", "tp"), None),
        P("grp", None),
        P(),
        P("grp", None),
        P("grp", None),
        P(("side", "grp", "tp"), None, None),
        P(("side", "grp", "tp"), None, None),
    )
    out_specs = P("grp", ("side", "tp"))
    return jax.shard_map(body, mesh=mesh, in_specs=in_specs, out_specs=out_specs, check_vma=False)
```

```python
import functools
import math

import jax
import jax.numpy as jnp
from jax import lax
from jax.experimental import pallas as pl
from jax.experimental.pallas import tpu as pltpu
from jax.sharding import PartitionSpec as P

HD = 128
TOPK = 8
SLOTS = 4
NEG = -1e30
F32 = jnp.float32
BF16 = jnp.bfloat16
MESH = pl.DeviceIdType.MESH


def kernel(
    dims,
    len_hbm,
    q_hbm,
    kv_hbm,
    ow_hbm,
    resid_hbm,
    gain_hbm,
    ids_hbm,
    gates_hbm,
    wgu_hbm,
    wd_hbm,
    out_ref,
    len_ref,
    gain_v,
    ids_v,
    gates_v,
    q_v,
    kv_v,
    ow_v,
    res_v,
    wgu_v,
    wd_v,
    qf,
    num,
    lse,
    pick,
    mix,
    a_send,
    a_recv,
    b_send,
    b_recv,
    d_send,
    d_recv,
    e_send,
    e_recv,
    small_sem,
    kv_sem,
    in_sem,
    send_sem,
    recv_sem,
):
    sides, grps, tps, parts = dims
    members = sides * tps
    experts = members * grps
    rows = q_v.shape[0]
    heads = q_v.shape[1] // HD
    span = kv_v.shape[1]
    width = ow_v.shape[1]
    mine_rows = rows * heads // parts
    inner = wd_v.shape[0]
    side = lax.axis_index("side")
    grp = lax.axis_index("grp")
    tp = lax.axis_index("tp")
    member = side * tps + tp
    part = lax.rem(tp, parts)
    head_group = tp // parts
    groups = tps // parts
    mine_expert = (side * grps + grp) * tps + tp

    grp_low = 4 if grps % 4 == 0 else grps
    grp_high = grps // grp_low
    side_at = [lax.rem(side + d, sides) for d in range(sides)]
    grp_at = {}
    for hi in range(grp_high):
        for lo in range(grp_low):
            grp_at[hi, lo] = lax.rem(grp // grp_low + hi, grp_high) * grp_low + lax.rem(
                lax.rem(grp, grp_low) + lo, grp_low
            )
    tp_at = {}
    for hi in range(groups):
        for lo in range(parts):
            tp_at[hi, lo] = lax.rem(head_group + hi, groups) * parts + lax.rem(part + lo, parts)

    def ring(d, size):
        return min(d, size - d)

    offsets = []
    for ds in range(sides):
        for gh, gl in grp_at:
            for th, tl in tp_at:
                if ds or gh or gl or th or tl:
                    far = 2 * gh + ring(gl, grp_low) + th + ring(tl, parts)
                    offsets.append((-far, ds, gh, gl, th, tl))
    offsets.sort()
    everyone = [(side_at[ds], grp_at[gh, gl], tp_at[th, tl]) for _, ds, gh, gl, th, tl in offsets]
    row_group = [
        (side_at[ds], grp, tp_at[th, tl]) for _, ds, gh, gl, th, tl in offsets if not (gh or gl)
    ]
    column = [(side, grp_at[gh, gl], tp) for _, ds, gh, gl, th, tl in offsets if not (ds or th or tl)]
    same_head = [
        (side, grp, tp_at[th, tl]) for _, ds, gh, gl, th, tl in offsets if not (ds or gh or gl or th)
    ]

    q_copy = pltpu.make_async_copy(
        q_hbm.at[:, pl.ds(pl.multiple_of(head_group * heads * HD, 128), heads * HD)], q_v, in_sem.at[0]
    )
    q_copy.start()
    len_copy = pltpu.make_async_copy(len_hbm, len_ref, small_sem.at[0])
    len_copy.start()
    kv_copies = []
    chunks = kv_sem.shape[0]
    per_chunk = rows // chunks
    for c in range(chunks):
        copy = pltpu.make_async_copy(
            kv_hbm.at[pl.ds(c * per_chunk, per_chunk), 0], kv_v.at[pl.ds(c * per_chunk, per_chunk)], kv_sem.at[c]
        )
        copy.start()
        kv_copies.append(copy)

    barrier = pltpu.get_barrier_semaphore()
    for device in column + row_group:
        pl.semaphore_signal(barrier, inc=1, device_id=device, device_id_type=MESH)

    ids_copy = pltpu.make_async_copy(ids_hbm, ids_v, small_sem.at[1])
    ids_copy.start()
    gates_copy = pltpu.make_async_copy(gates_hbm, gates_v, small_sem.at[2])
    gates_copy.start()
    gain_copy = pltpu.make_async_copy(gain_hbm, gain_v, small_sem.at[3])
    gain_copy.start()
    ow_copy = pltpu.make_async_copy(ow_hbm, ow_v, in_sem.at[1])
    ow_copy.start()
    res_copy = pltpu.make_async_copy(
        resid_hbm.at[:, pl.ds(pl.multiple_of(member * 128, 128), 128)], res_v, in_sem.at[2]
    )
    res_copy.start()
    wgu_copy = pltpu.make_async_copy(wgu_hbm.at[0], wgu_v, in_sem.at[3])
    wgu_copy.start()
    wd_copy = pltpu.make_async_copy(wd_hbm.at[0], wd_v, in_sem.at[4])
    wd_copy.start()

    ids_copy.wait()
    gates_copy.wait()
    eye = (
        lax.broadcasted_iota(jnp.int32, (TOPK, TOPK), 0) == lax.broadcasted_iota(jnp.int32, (TOPK, TOPK), 1)
    ).astype(BF16)

    def flipped(value):
        return lax.dot_general(value.astype(BF16), eye, (((0,), (0,)), ((), ())), preferred_element_type=F32)

    gates_t = gates_v[...]
    gates_high = gates_t.astype(BF16).astype(F32)
    gates_middle = (gates_t - gates_high).astype(BF16).astype(F32)
    ids = flipped(ids_v[...].astype(F32))
    gates = flipped(gates_high) + (flipped(gates_middle) + flipped(gates_t - gates_high - gates_middle))
    col = lax.broadcasted_iota(jnp.int32, (rows, experts * SLOTS), 1)
    expert = (col // SLOTS).astype(F32)
    hit = jnp.zeros((rows, experts * SLOTS), F32)
    gate_cols = jnp.zeros((rows, experts * SLOTS), F32)
    for k in range(TOPK):
        same = ids[:, k : k + 1] == expert
        hit = jnp.where(same, 1.0, hit)
        gate_cols = jnp.where(same, gates[:, k : k + 1], gate_cols)
    below = (
        lax.broadcasted_iota(jnp.int32, (rows, rows), 1) < lax.broadcasted_iota(jnp.int32, (rows, rows), 0)
    ).astype(BF16)
    rank = jnp.dot(below, hit.astype(BF16), preferred_element_type=F32)
    placed = jnp.where(rank == (col % SLOTS).astype(F32), hit, 0.0)
    same_row = (
        lax.broadcasted_iota(jnp.int32, (rows, rows), 1) == lax.broadcasted_iota(jnp.int32, (rows, rows), 0)
    ).astype(BF16)
    pick[...] = lax.dot_general(
        placed.astype(BF16), same_row, (((0,), (0,)), ((), ())), preferred_element_type=F32
    ).astype(BF16)
    combine = placed * gate_cols
    combine_high = combine.astype(BF16).astype(F32)
    mix[...] = jnp.concatenate([combine_high, combine - combine_high], axis=0).astype(BF16)

    q_copy.wait()
    for j in range(heads):
        qf[j * rows : (j + 1) * rows, :] = q_v[:, j * HD : (j + 1) * HD].astype(F32)
    len_copy.wait()
    first = part * span
    position = first + lax.broadcasted_iota(jnp.int32, (heads, span), 1)
    scale = 1.0 / math.sqrt(HD)

    def attend_scores(batch):
        made = []
        for r in batch:
            query = qf[pl.ds(r, heads, stride=rows), :].astype(BF16)
            made.append(
                lax.dot_general(query, kv_v[r, :, :HD], (((1,), (1,)), ((), ())), preferred_element_type=F32)
            )
        return made

    def attend_values(batch, made):
        valids = [position < len_ref[r] for r in batch]
        made = [jnp.where(valid, score * scale, NEG) for valid, score in zip(valids, made)]
        tops = [jnp.max(score, axis=1, keepdims=True) for score in made]
        weights = [
            jnp.where(valid, jnp.exp(score - top), 0.0) for valid, score, top in zip(valids, made, tops)
        ]
        totals = [jnp.sum(weight, axis=1, keepdims=True) for weight in weights]
        results = [
            jnp.dot(weight.astype(BF16), kv_v[r, :, HD:], preferred_element_type=F32)
            for r, weight in zip(batch, weights)
        ]
        for r, top, total, value in zip(batch, tops, totals, results):
            some = total > 0.0
            safe = jnp.where(some, total, 1.0)
            num[pl.ds(r, heads, stride=rows), :] = value * (1.0 / safe)
            lse[pl.ds(r, heads, stride=rows), :] = jnp.broadcast_to(
                jnp.where(some, top + jnp.log(safe), NEG), (heads, HD)
            )

    batches = [range(c * per_chunk, (c + 1) * per_chunk) for c in range(chunks)]
    ready = None
    for c in range(chunks):
        kv_copies[c].wait()
        made = attend_scores(batches[c])
        if ready is not None:
            attend_values(batches[c - 1], ready)
        ready = made
    attend_values(batches[-1], ready)

    diagonal = lax.broadcasted_iota(jnp.int32, (mine_rows, HD), 0) == lax.broadcasted_iota(
        jnp.int32, (mine_rows, HD), 1
    )
    line = lax.broadcasted_iota(jnp.int32, (16, HD), 0)
    for p in range(parts):
        block = slice(p * mine_rows, (p + 1) * mine_rows)
        a_send[p, :mine_rows, :] = num[block, :].astype(BF16)
        stat = jnp.sum(jnp.where(diagonal, lse[block, :], 0.0), axis=0, keepdims=True)
        high = stat.astype(BF16).astype(F32)
        middle_word = (stat - high).astype(BF16).astype(F32)
        low = stat - high - middle_word
        words = jnp.where(line == 0, high, jnp.where(line == 1, middle_word, jnp.where(line == 2, low, 0.0)))
        a_send[p, mine_rows:, :] = words.astype(BF16)

    pl.semaphore_wait(barrier, members + grps - 2)

    def remote(src, dst, index, device):
        return pltpu.make_async_remote_copy(
            src_ref=src,
            dst_ref=dst,
            send_sem=send_sem.at[index],
            recv_sem=recv_sem.at[index],
            device_id=device,
            device_id_type=MESH,
        )

    for i, device in enumerate(same_head):
        remote(a_send.at[lax.rem(device[2], parts)], a_recv.at[i], 0, device).start()
    done_a = remote(a_send.at[pl.ds(0, parts - 1)], a_recv, 0, same_head[0])
    own = pl.ds(pl.multiple_of(part * mine_rows, 8), mine_rows)
    values = [num[own, :]]
    levels = [lse[own, :][:, 0:1]]
    done_a.wait_recv()
    for d in range(parts - 1):
        values.append(a_recv[d, :mine_rows, :].astype(F32))
        row = jnp.sum(a_recv[d, mine_rows:, :].astype(F32), axis=0, keepdims=True)
        levels.append(jnp.sum(jnp.where(diagonal, row, 0.0), axis=1, keepdims=True))
    peak = functools.reduce(jnp.maximum, levels)
    shares = [jnp.exp(level - peak) for level in levels]
    whole = functools.reduce(jnp.add, shares)
    merged = functools.reduce(jnp.add, [v * s for v, s in zip(values, shares)]) * (1.0 / whole)
    per_member = mine_rows // rows
    attended = jnp.concatenate(
        [merged[i * rows : (i + 1) * rows, :] for i in range(per_member)], axis=1
    ).astype(BF16)

    ow_copy.wait()
    projected = jnp.dot(attended, ow_v[...], preferred_element_type=F32)
    for j in range(members):
        b_send[j, :, :] = projected[:, j * 128 : (j + 1) * 128].astype(BF16)
    for i, device in enumerate(row_group):
        remote(b_send.at[device[0] * tps + device[2]], b_recv.at[i], 1, device).start()
    done_b = remote(b_send.at[pl.ds(0, members - 1)], b_recv, 1, row_group[0])
    res_copy.wait()
    acc = res_v[...].astype(F32) + b_send[member, :, :].astype(F32)
    done_b.wait_recv()
    for d in range(members - 1):
        acc = acc + b_recv[d, :, :].astype(F32)
    middle = acc.astype(BF16)

    chosen = jnp.dot(pick[...], middle, preferred_element_type=F32).astype(BF16)
    d_send[...] = chosen.reshape(experts, SLOTS, 128)
    slot = member * grps + grp
    for device in everyone:
        remote(d_send.at[(device[0] * grps + device[1]) * tps + device[2]], d_recv.at[slot], 2, device).start()
    d_recv[slot, :, :] = d_send[mine_expert, :, :]
    done_d = remote(d_send.at[pl.ds(0, experts - 1)], d_recv.at[pl.ds(0, experts - 1)], 2, everyone[0])
    gain_copy.wait()
    wgu_copy.wait()
    done_d.wait_recv()
    pieces = [
        d_recv[j * grps : (j + 1) * grps, :, :].reshape(grps * SLOTS, 128).astype(F32) for j in range(members)
    ]
    square = functools.reduce(jnp.add, [piece * piece for piece in pieces])
    inv_rms = lax.rsqrt(jnp.sum(square, axis=1, keepdims=True) * (1.0 / width) + 1e-6)
    normed = jnp.concatenate(
        [(piece * inv_rms * gain_v[j : j + 1, :]).astype(BF16) for j, piece in enumerate(pieces)], axis=1
    )
    both = jnp.dot(normed, wgu_v[...], preferred_element_type=F32)
    gate = both[:, :inner]
    act = (gate / (1.0 + jnp.exp(-gate)) * both[:, inner:]).astype(BF16)
    wd_copy.wait()
    produced = jnp.dot(act, wd_v[...], preferred_element_type=F32).astype(BF16)

    for j in range(members):
        e_send[:, j, :, :] = produced[:, j * 128 : (j + 1) * 128].reshape(grps, SLOTS, 128)
    for device in everyone:
        remote(e_send.at[device[1], device[0] * tps + device[2]], e_recv.at[mine_expert], 3, device).start()
    e_recv[mine_expert, :, :] = e_send[grp, member, :, :]
    done_e = remote(e_recv.at[pl.ds(0, experts - 1)], e_recv.at[pl.ds(0, experts - 1)], 3, everyone[0])
    done_e.wait_recv()
    returned = e_recv[...].reshape(experts * SLOTS, 128)
    gated = jnp.dot(mix[...], returned, preferred_element_type=F32)
    out_ref[...] = (middle.astype(F32) + (gated[:rows, :] + gated[rows:, :])).astype(BF16)
    for done in (done_a, done_b, done_d, done_e):
        done.wait_send()


def body(queries, kv_cache, lengths, out_weight, resid, norm_gain, expert_ids, expert_gates, w_gate_up, w_down):
    sides, grps, tps = lax.axis_size("side"), lax.axis_size("grp"), lax.axis_size("tp")
    members = sides * tps
    experts = members * grps
    rows = queries.shape[0]
    parts = 4
    heads = 8
    span = kv_cache.shape[2]
    width = out_weight.shape[1]
    mine_rows = rows * heads // parts
    anywhere = pl.BlockSpec(memory_space=pl.ANY)
    return pl.pallas_call(
        functools.partial(kernel, (sides, grps, tps, parts)),
        out_shape=pltpu.VMEM((rows, width // members), BF16),
        in_specs=[anywhere] * 10,
        out_specs=pl.BlockSpec(memory_space=pltpu.VMEM),
        scratch_shapes=[
            pltpu.SMEM((rows,), jnp.int32),
            pltpu.VMEM((members, width // members), F32),
            pltpu.VMEM((TOPK, rows), jnp.int32),
            pltpu.VMEM((TOPK, rows), F32),
            pltpu.VMEM((rows, heads * HD), BF16),
            pltpu.VMEM((rows, span, 2 * HD), BF16),
            pltpu.VMEM(out_weight.shape, BF16),
            pltpu.VMEM((rows, 128), BF16),
            pltpu.VMEM(w_gate_up.shape[1:], BF16),
            pltpu.VMEM(w_down.shape[1:], BF16),
            pltpu.VMEM((rows * heads, HD), F32),
            pltpu.VMEM((rows * heads, HD), F32),
            pltpu.VMEM((rows * heads, HD), F32),
            pltpu.VMEM((experts * SLOTS, rows), BF16),
            pltpu.VMEM((2 * rows, experts * SLOTS), BF16),
            pltpu.VMEM((parts, mine_rows + 16, HD), BF16),
            pltpu.VMEM((parts - 1, mine_rows + 16, HD), BF16),
            pltpu.VMEM((members, rows, 128), BF16),
            pltpu.VMEM((members - 1, rows, 128), BF16),
            pltpu.VMEM((experts, SLOTS, 128), BF16),
            pltpu.VMEM((experts, SLOTS, 128), BF16),
            pltpu.VMEM((grps, members, SLOTS, 128), BF16),
            pltpu.VMEM((experts, SLOTS, 128), BF16),
            pltpu.SemaphoreType.DMA((4,)),
            pltpu.SemaphoreType.DMA((2,)),
            pltpu.SemaphoreType.DMA((5,)),
            pltpu.SemaphoreType.DMA((4,)),
            pltpu.SemaphoreType.DMA((4,)),
        ],
        compiler_params=pltpu.CompilerParams(
            collective_id=0, has_side_effects=True, vmem_limit_bytes=56 * 1024 * 1024
        ),
        name="layer",
    )(
        lengths,
        queries,
        kv_cache,
        out_weight,
        resid,
        norm_gain.reshape(members, width // members),
        expert_ids.T,
        expert_gates.T,
        w_gate_up,
        w_down,
    )


def solution(mesh):
    in_specs = (
        P("grp", "side"),
        P("grp", ("side", "tp"), None, None),
        P("grp"),
        P(("side", "tp"), None),
        P("grp", None),
        P(),
        P("grp", None),
        P("grp", None),
        P(("side", "grp", "tp"), None, None),
        P(("side", "grp", "tp"), None, None),
    )
    out_specs = P("grp", ("side", "tp"))
    return jax.shard_map(body, mesh=mesh, in_specs=in_specs, out_specs=out_specs, check_vma=False)
```

```python
import functools
import math

import jax
import jax.numpy as jnp
from jax import lax
from jax.experimental import pallas as pl
from jax.experimental.pallas import tpu as pltpu
from jax.sharding import PartitionSpec as P

HD = 128
TOPK = 8
SLOTS = 4
NEG = -1e30
F32 = jnp.float32
BF16 = jnp.bfloat16
MESH = pl.DeviceIdType.MESH


def kernel(
    dims,
    len_hbm,
    q_hbm,
    kv_hbm,
    ow_hbm,
    resid_hbm,
    gain_hbm,
    ids_hbm,
    gates_hbm,
    wgu_hbm,
    wd_hbm,
    out_ref,
    len_ref,
    gain_v,
    ids_v,
    gates_v,
    q_v,
    kv_v,
    ow_v,
    res_v,
    wgu_v,
    wd_v,
    qf,
    num,
    lse,
    pick,
    mix,
    a_send,
    a_recv,
    b_send,
    b_recv,
    d_send,
    d_recv,
    e_send,
    e_recv,
    small_sem,
    kv_sem,
    in_sem,
    send_sem,
    recv_sem,
    band_sem,
):
    sides, grps, tps, parts = dims
    members = sides * tps
    experts = members * grps
    rows = q_v.shape[0]
    heads = q_v.shape[1] // HD
    span = kv_v.shape[1]
    width = ow_v.shape[1]
    mine_rows = rows * heads // parts
    inner = wd_v.shape[0]
    side = lax.axis_index("side")
    grp = lax.axis_index("grp")
    tp = lax.axis_index("tp")
    member = side * tps + tp
    part = lax.rem(tp, parts)
    head_group = tp // parts
    groups = tps // parts
    mine_expert = (side * grps + grp) * tps + tp

    grp_low = 4 if grps % 4 == 0 else grps
    grp_high = grps // grp_low
    side_at = [lax.rem(side + d, sides) for d in range(sides)]
    grp_at = {}
    for hi in range(grp_high):
        for lo in range(grp_low):
            grp_at[hi, lo] = lax.rem(grp // grp_low + hi, grp_high) * grp_low + lax.rem(
                lax.rem(grp, grp_low) + lo, grp_low
            )
    tp_at = {}
    for hi in range(groups):
        for lo in range(parts):
            tp_at[hi, lo] = lax.rem(head_group + hi, groups) * parts + lax.rem(part + lo, parts)

    def ring(d, size):
        return min(d, size - d)

    offsets = []
    for ds in range(sides):
        for gh, gl in grp_at:
            for th, tl in tp_at:
                if ds or gh or gl or th or tl:
                    far = (1 if th else 2 * gh) + ring(gl, grp_low) + ring(tl, parts)
                    offsets.append((-far, ds, gh, gl, th, tl))
    offsets.sort()

    def device_at(ds, gh, gl, th, tl):
        return side_at[ds], grp_at[gh, gl], tp_at[th, tl]

    everyone = [o[1:] for o in offsets]
    row_group = [o for o in everyone if not (o[1] or o[2])]
    piece_order = sorted(
        [(ds, th, tl) for ds in range(sides) for th, tl in tp_at], key=lambda o: (ring(o[2], parts), o)
    )
    group_order = sorted(grp_at)
    piece_index = {o: i for i, o in enumerate(piece_order)}
    group_index = {o: i for i, o in enumerate(group_order)}
    piece_member = [side_at[ds] * tps + tp_at[th, tl] for ds, th, tl in piece_order]
    bands = sorted({ring(o[2], parts) for o in piece_order})
    band_pieces = {b: [i for i, o in enumerate(piece_order) if ring(o[2], parts) == b] for b in bands}

    def close(ds, gh, gl, th, tl):
        if gh:
            return th and not (ds or tl)
        if gl:
            return not (ds or th or tl)
        return not (tl and (ds or th))

    near = [o for o in everyone if close(*o)]
    same_head = [device_at(*o) for o in everyone if not (o[0] or o[1] or o[2] or o[3])]

    barrier = pltpu.get_barrier_semaphore()
    for o in near:
        pl.semaphore_signal(barrier, inc=1, device_id=device_at(*o), device_id_type=MESH)

    q_copy = pltpu.make_async_copy(
        q_hbm.at[:, pl.ds(pl.multiple_of(head_group * heads * HD, 128), heads * HD)], q_v, in_sem.at[0]
    )
    q_copy.start()
    len_copy = pltpu.make_async_copy(len_hbm, len_ref, small_sem.at[0])
    len_copy.start()
    kv_copies = []
    chunks = kv_sem.shape[0]
    per_chunk = rows // chunks
    for c in range(chunks):
        copy = pltpu.make_async_copy(
            kv_hbm.at[pl.ds(c * per_chunk, per_chunk), 0], kv_v.at[pl.ds(c * per_chunk, per_chunk)], kv_sem.at[c]
        )
        copy.start()
        kv_copies.append(copy)

    ids_copy = pltpu.make_async_copy(ids_hbm, ids_v, small_sem.at[1])
    ids_copy.start()
    gates_copy = pltpu.make_async_copy(gates_hbm, gates_v, small_sem.at[2])
    gates_copy.start()
    gain_copy = pltpu.make_async_copy(gain_hbm, gain_v, small_sem.at[3])
    gain_copy.start()
    ow_copy = pltpu.make_async_copy(ow_hbm, ow_v, in_sem.at[1])
    wgu_copy = pltpu.make_async_copy(wgu_hbm.at[0], wgu_v, in_sem.at[3])
    wd_copy = pltpu.make_async_copy(wd_hbm.at[0], wd_v, in_sem.at[4])
    ow_copy.start()
    res_copy = pltpu.make_async_copy(
        resid_hbm.at[:, pl.ds(pl.multiple_of(member * 128, 128), 128)], res_v, in_sem.at[2]
    )
    res_copy.start()

    ids_copy.wait()
    gates_copy.wait()
    eye = (
        lax.broadcasted_iota(jnp.int32, (TOPK, TOPK), 0) == lax.broadcasted_iota(jnp.int32, (TOPK, TOPK), 1)
    ).astype(BF16)

    def flipped(value):
        return lax.dot_general(value.astype(BF16), eye, (((0,), (0,)), ((), ())), preferred_element_type=F32)

    gates_t = gates_v[...]
    gates_high = gates_t.astype(BF16).astype(F32)
    gates_middle = (gates_t - gates_high).astype(BF16).astype(F32)
    ids = flipped(ids_v[...].astype(F32))
    gates = flipped(gates_high) + (flipped(gates_middle) + flipped(gates_t - gates_high - gates_middle))
    col = lax.broadcasted_iota(jnp.int32, (rows, experts * SLOTS), 1)
    expert = (col // SLOTS).astype(F32)
    hit = jnp.zeros((rows, experts * SLOTS), F32)
    gate_cols = jnp.zeros((rows, experts * SLOTS), F32)
    for k in range(TOPK):
        same = ids[:, k : k + 1] == expert
        hit = jnp.where(same, 1.0, hit)
        gate_cols = jnp.where(same, gates[:, k : k + 1], gate_cols)
    below = (
        lax.broadcasted_iota(jnp.int32, (rows, rows), 1) < lax.broadcasted_iota(jnp.int32, (rows, rows), 0)
    ).astype(BF16)
    rank = jnp.dot(below, hit.astype(BF16), preferred_element_type=F32)
    placed = jnp.where(rank == (col % SLOTS).astype(F32), hit, 0.0)
    same_row = (
        lax.broadcasted_iota(jnp.int32, (rows, rows), 1) == lax.broadcasted_iota(jnp.int32, (rows, rows), 0)
    ).astype(BF16)
    pick[...] = lax.dot_general(
        placed.astype(BF16), same_row, (((0,), (0,)), ((), ())), preferred_element_type=F32
    ).astype(BF16)
    combine = placed * gate_cols
    combine_high = combine.astype(BF16).astype(F32)
    mix[...] = jnp.concatenate([combine_high, combine - combine_high], axis=0).astype(BF16)

    q_copy.wait()
    for j in range(heads):
        qf[j * rows : (j + 1) * rows, :] = q_v[:, j * HD : (j + 1) * HD].astype(F32)
    len_copy.wait()
    first = part * span
    position = first + lax.broadcasted_iota(jnp.int32, (heads, span), 1)
    scale = 1.0 / math.sqrt(HD)

    def attend_scores(batch):
        made = []
        for r in batch:
            query = qf[pl.ds(r, heads, stride=rows), :].astype(BF16)
            made.append(
                lax.dot_general(query, kv_v[r, :, :HD], (((1,), (1,)), ((), ())), preferred_element_type=F32)
            )
        return made

    def attend_values(batch, made):
        valids = [position < len_ref[r] for r in batch]
        made = [jnp.where(valid, score * scale, NEG) for valid, score in zip(valids, made)]
        tops = [jnp.max(score, axis=1, keepdims=True) for score in made]
        weights = [
            jnp.where(valid, jnp.exp(score - top), 0.0) for valid, score, top in zip(valids, made, tops)
        ]
        totals = [jnp.sum(weight, axis=1, keepdims=True) for weight in weights]
        results = [
            jnp.dot(weight.astype(BF16), kv_v[r, :, HD:], preferred_element_type=F32)
            for r, weight in zip(batch, weights)
        ]
        for r, top, total, value in zip(batch, tops, totals, results):
            some = total > 0.0
            safe = jnp.where(some, total, 1.0)
            num[pl.ds(r, heads, stride=rows), :] = value * (1.0 / safe)
            lse[pl.ds(r, heads, stride=rows), :] = jnp.broadcast_to(
                jnp.where(some, top + jnp.log(safe), NEG), (heads, HD)
            )

    batches = [range(c * per_chunk, (c + 1) * per_chunk) for c in range(chunks)]
    ready = None
    for c in range(chunks):
        kv_copies[c].wait()
        made = attend_scores(batches[c])
        if ready is not None:
            attend_values(batches[c - 1], ready)
        ready = made
    attend_values(batches[-1], ready)

    diagonal = lax.broadcasted_iota(jnp.int32, (mine_rows, HD), 0) == lax.broadcasted_iota(
        jnp.int32, (mine_rows, HD), 1
    )
    line = lax.broadcasted_iota(jnp.int32, (16, HD), 0)
    for p in range(parts):
        block = slice(p * mine_rows, (p + 1) * mine_rows)
        a_send[p, :mine_rows, :] = num[block, :].astype(BF16)
        stat = jnp.sum(jnp.where(diagonal, lse[block, :], 0.0), axis=0, keepdims=True)
        high = stat.astype(BF16).astype(F32)
        middle_word = (stat - high).astype(BF16).astype(F32)
        low = stat - high - middle_word
        words = jnp.where(line == 0, high, jnp.where(line == 1, middle_word, jnp.where(line == 2, low, 0.0)))
        a_send[p, mine_rows:, :] = words.astype(BF16)

    pl.semaphore_wait(barrier, len(near))

    def remote(src, dst, sent, received, device):
        return pltpu.make_async_remote_copy(
            src_ref=src,
            dst_ref=dst,
            send_sem=sent,
            recv_sem=received,
            device_id=device,
            device_id_type=MESH,
        )

    for i, device in enumerate(same_head):
        remote(a_send.at[lax.rem(device[2], parts)], a_recv.at[i], send_sem.at[0], recv_sem.at[0], device).start()
    done_a = remote(a_send.at[pl.ds(0, parts - 1)], a_recv, send_sem.at[0], recv_sem.at[0], same_head[0])
    for i, block in enumerate(piece_member):
        there = pl.ds(pl.multiple_of(block * 128, 128), 128)
        pltpu.make_async_copy(wgu_hbm.at[0, there, :], wgu_v.at[pl.ds(i * 128, 128), :], in_sem.at[3]).start()
    own = pl.ds(pl.multiple_of(part * mine_rows, 8), mine_rows)
    values = [num[own, :]]
    levels = [lse[own, :][:, 0:1]]
    done_a.wait_recv()
    for d in range(parts - 1):
        values.append(a_recv[d, :mine_rows, :].astype(F32))
        row = jnp.sum(a_recv[d, mine_rows:, :].astype(F32), axis=0, keepdims=True)
        levels.append(jnp.sum(jnp.where(diagonal, row, 0.0), axis=1, keepdims=True))
    peak = functools.reduce(jnp.maximum, levels)
    shares = [jnp.exp(level - peak) for level in levels]
    whole = functools.reduce(jnp.add, shares)
    merged = functools.reduce(jnp.add, [v * s for v, s in zip(values, shares)]) * (1.0 / whole)
    per_member = mine_rows // rows
    attended = jnp.concatenate(
        [merged[i * rows : (i + 1) * rows, :] for i in range(per_member)], axis=1
    ).astype(BF16)

    ow_copy.wait()
    projected = jnp.dot(attended, ow_v[...], preferred_element_type=F32)
    for j in range(members):
        b_send[j, :, :] = projected[:, j * 128 : (j + 1) * 128].astype(BF16)
    for i, o in enumerate(row_group):
        device = device_at(*o)
        remote(b_send.at[device[0] * tps + device[2]], b_recv.at[i], send_sem.at[1], recv_sem.at[1], device).start()
    done_b = remote(
        b_send.at[pl.ds(0, members - 1)], b_recv, send_sem.at[1], recv_sem.at[1], device_at(*row_group[0])
    )
    for i, block in enumerate(piece_member):
        there = pl.ds(pl.multiple_of(block * 128, 128), 128)
        pltpu.make_async_copy(wd_hbm.at[0, :, there], wd_v.at[:, pl.ds(i * 128, 128)], in_sem.at[4]).start()
    res_copy.wait()
    acc = res_v[...].astype(F32) + b_send[member, :, :].astype(F32)
    done_b.wait_recv()
    for d in range(members - 1):
        acc = acc + b_recv[d, :, :].astype(F32)
    middle = acc.astype(BF16)

    chosen = jnp.dot(pick[...], middle, preferred_element_type=F32).astype(BF16)
    d_send[...] = chosen.reshape(experts, SLOTS, 128)
    some_device = device_at(*everyone[0])
    for ds, gh, gl, th, tl in everyone:
        device = device_at(ds, gh, gl, th, tl)
        slot = piece_index[ds, th, (parts - tl) % parts] * grps + group_index[gh, (grp_low - gl) % grp_low]
        remote(
            d_send.at[(device[0] * grps + device[1]) * tps + device[2]],
            d_recv.at[slot],
            send_sem.at[2],
            band_sem.at[ring(tl, parts)],
            device,
        ).start()
    d_recv[0, :, :] = d_send[mine_expert, :, :]
    gain_copy.wait()
    wgu_copy.wait()
    both = None
    square = None
    for band in bands:
        members_in = band_pieces[band]
        count = len(members_in) * grps - (1 if band == 0 else 0)
        some = pl.ds(0, count)
        remote(d_recv.at[some], d_recv.at[some], send_sem.at[2], band_sem.at[band], some_device).wait_recv()
        inputs = []
        for i in members_in:
            piece = d_recv[i * grps : (i + 1) * grps, :, :].reshape(grps * SLOTS, 128).astype(F32)
            square = piece * piece if square is None else square + piece * piece
            inputs.append((piece * gain_v[pl.ds(piece_member[i], 1), :]).astype(BF16))
        partial = jnp.dot(
            jnp.concatenate(inputs, axis=1),
            wgu_v[members_in[0] * 128 : (members_in[-1] + 1) * 128, :],
            preferred_element_type=F32,
        )
        both = partial if both is None else both + partial
    done_d = remote(
        d_send.at[pl.ds(0, experts - 1)], d_recv.at[pl.ds(0, experts - 1)], send_sem.at[2], band_sem.at[0], some_device
    )
    inv_rms = lax.rsqrt(jnp.sum(square, axis=1, keepdims=True) * (1.0 / width) + 1e-6)
    both = both * inv_rms
    gate = both[:, :inner]
    act = (gate / (1.0 + jnp.exp(-gate)) * both[:, inner:]).astype(BF16)
    wd_copy.wait()

    for band in reversed(bands):
        low, high = band_pieces[band][0], band_pieces[band][-1] + 1
        produced = jnp.dot(act, wd_v[:, low * 128 : high * 128], preferred_element_type=F32).astype(BF16)
        for p in range(low, high):
            e_send[:, p, :, :] = produced[:, (p - low) * 128 : (p - low + 1) * 128].reshape(grps, SLOTS, 128)
        for ds, gh, gl, th, tl in everyone:
            p = piece_index[ds, th, tl]
            if low <= p < high:
                remote(
                    e_send.at[group_index[gh, gl], p],
                    e_recv.at[mine_expert],
                    send_sem.at[3],
                    recv_sem.at[2],
                    device_at(ds, gh, gl, th, tl),
                ).start()
    e_recv[mine_expert, :, :] = e_send[0, 0, :, :]
    some = pl.ds(0, experts - 1)
    done_e = remote(e_recv.at[some], e_recv.at[some], send_sem.at[3], recv_sem.at[2], some_device)
    done_e.wait_recv()
    returned = e_recv[...].reshape(experts * SLOTS, 128)
    gated = jnp.dot(mix[...], returned, preferred_element_type=F32)
    out_ref[...] = (middle.astype(F32) + (gated[:rows, :] + gated[rows:, :])).astype(BF16)
    for done in (done_a, done_b, done_d, done_e):
        done.wait_send()


def body(queries, kv_cache, lengths, out_weight, resid, norm_gain, expert_ids, expert_gates, w_gate_up, w_down):
    sides, grps, tps = lax.axis_size("side"), lax.axis_size("grp"), lax.axis_size("tp")
    members = sides * tps
    experts = members * grps
    rows = queries.shape[0]
    parts = 4
    heads = 8
    span = kv_cache.shape[2]
    width = out_weight.shape[1]
    mine_rows = rows * heads // parts
    anywhere = pl.BlockSpec(memory_space=pl.ANY)
    return pl.pallas_call(
        functools.partial(kernel, (sides, grps, tps, parts)),
        out_shape=pltpu.VMEM((rows, width // members), BF16),
        in_specs=[anywhere] * 10,
        out_specs=pl.BlockSpec(memory_space=pltpu.VMEM),
        scratch_shapes=[
            pltpu.SMEM((rows,), jnp.int32),
            pltpu.VMEM((members, width // members), F32),
            pltpu.VMEM((TOPK, rows), jnp.int32),
            pltpu.VMEM((TOPK, rows), F32),
            pltpu.VMEM((rows, heads * HD), BF16),
            pltpu.VMEM((rows, span, 2 * HD), BF16),
            pltpu.VMEM(out_weight.shape, BF16),
            pltpu.VMEM((rows, 128), BF16),
            pltpu.VMEM(w_gate_up.shape[1:], BF16),
            pltpu.VMEM(w_down.shape[1:], BF16),
            pltpu.VMEM((rows * heads, HD), F32),
            pltpu.VMEM((rows * heads, HD), F32),
            pltpu.VMEM((rows * heads, HD), F32),
            pltpu.VMEM((experts * SLOTS, rows), BF16),
            pltpu.VMEM((2 * rows, experts * SLOTS), BF16),
            pltpu.VMEM((parts, mine_rows + 16, HD), BF16),
            pltpu.VMEM((parts - 1, mine_rows + 16, HD), BF16),
            pltpu.VMEM((members, rows, 128), BF16),
            pltpu.VMEM((members - 1, rows, 128), BF16),
            pltpu.VMEM((experts, SLOTS, 128), BF16),
            pltpu.VMEM((experts, SLOTS, 128), BF16),
            pltpu.VMEM((grps, members, SLOTS, 128), BF16),
            pltpu.VMEM((experts, SLOTS, 128), BF16),
            pltpu.SemaphoreType.DMA((4,)),
            pltpu.SemaphoreType.DMA((2,)),
            pltpu.SemaphoreType.DMA((5,)),
            pltpu.SemaphoreType.DMA((4,)),
            pltpu.SemaphoreType.DMA((3,)),
            pltpu.SemaphoreType.DMA((3,)),
        ],
        compiler_params=pltpu.CompilerParams(
            collective_id=0, has_side_effects=True, vmem_limit_bytes=56 * 1024 * 1024
        ),
        name="layer",
    )(
        lengths,
        queries,
        kv_cache,
        out_weight,
        resid,
        norm_gain.reshape(members, width // members),
        expert_ids.T,
        expert_gates.T,
        w_gate_up,
        w_down,
    )


def solution(mesh):
    in_specs = (
        P("grp", "side"),
        P("grp", ("side", "tp"), None, None),
        P("grp"),
        P(("side", "tp"), None),
        P("grp", None),
        P(),
        P("grp", None),
        P("grp", None),
        P(("side", "grp", "tp"), None, None),
        P(("side", "grp", "tp"), None, None),
    )
    out_specs = P("grp", ("side", "tp"))
    return jax.shard_map(body, mesh=mesh, in_specs=in_specs, out_specs=out_specs, check_vma=False)
```

```python
import functools
import math

import jax
import jax.numpy as jnp
from jax import lax
from jax.experimental import pallas as pl
from jax.experimental.pallas import tpu as pltpu
from jax.sharding import PartitionSpec as P

HD = 128
TOPK = 8
SLOTS = 4
NEG = -1e30
F32 = jnp.float32
BF16 = jnp.bfloat16
MESH = pl.DeviceIdType.MESH


def kernel(
    dims,
    len_hbm,
    q_hbm,
    kv_hbm,
    ow_hbm,
    resid_hbm,
    gain_hbm,
    ids_hbm,
    gates_hbm,
    wgu_hbm,
    wd_hbm,
    out_ref,
    len_ref,
    gain_v,
    ids_v,
    gates_v,
    q_v,
    kv_v,
    ow_v,
    res_v,
    wgu_v,
    wd_v,
    qf,
    num,
    lse,
    pick,
    mix,
    a_send,
    a_recv,
    b_send,
    b_recv,
    d_send,
    d_recv,
    e_send,
    e_recv,
    small_sem,
    kv_sem,
    in_sem,
    send_sem,
    recv_sem,
    band_sem,
    hello_sem,
):
    sides, grps, tps, parts = dims
    members = sides * tps
    experts = members * grps
    rows = q_v.shape[0]
    heads = q_v.shape[1] // HD
    span = kv_v.shape[1]
    width = ow_v.shape[1]
    mine_rows = rows * heads // parts
    inner = wd_v.shape[0]
    side = lax.axis_index("side")
    grp = lax.axis_index("grp")
    tp = lax.axis_index("tp")
    member = side * tps + tp
    part = lax.rem(tp, parts)
    head_group = tp // parts
    groups = tps // parts
    mine_expert = (side * grps + grp) * tps + tp

    grp_low = 4 if grps % 4 == 0 else grps
    grp_high = grps // grp_low
    side_at = [lax.rem(side + d, sides) for d in range(sides)]
    grp_at = {}
    for hi in range(grp_high):
        for lo in range(grp_low):
            grp_at[hi, lo] = lax.rem(grp // grp_low + hi, grp_high) * grp_low + lax.rem(
                lax.rem(grp, grp_low) + lo, grp_low
            )
    tp_at = {}
    for hi in range(groups):
        for lo in range(parts):
            tp_at[hi, lo] = lax.rem(head_group + hi, groups) * parts + lax.rem(part + lo, parts)

    def ring(d, size):
        return min(d, size - d)

    offsets = []
    for ds in range(sides):
        for gh, gl in grp_at:
            for th, tl in tp_at:
                if ds or gh or gl or th or tl:
                    far = (1 if th else 2 * gh) + ring(gl, grp_low) + ring(tl, parts)
                    offsets.append((-far, ds, gh, gl, th, tl))
    offsets.sort()

    def device_at(ds, gh, gl, th, tl):
        return side_at[ds], grp_at[gh, gl], tp_at[th, tl]

    everyone = [o[1:] for o in offsets]
    row_group = [o for o in everyone if not (o[1] or o[2])]
    piece_order = sorted(
        [(ds, th, tl) for ds in range(sides) for th, tl in tp_at], key=lambda o: (ring(o[2], parts), o)
    )
    group_order = sorted(grp_at)
    piece_index = {o: i for i, o in enumerate(piece_order)}
    group_index = {o: i for i, o in enumerate(group_order)}
    piece_member = [side_at[ds] * tps + tp_at[th, tl] for ds, th, tl in piece_order]
    bands = sorted({ring(o[2], parts) for o in piece_order})
    band_pieces = {b: [i for i, o in enumerate(piece_order) if ring(o[2], parts) == b] for b in bands}

    def close(ds, gh, gl, th, tl):
        if gh:
            return th and not (ds or tl) and gl != grp_low // 2
        if gl:
            return not (ds or th or tl)
        return not (tl and (ds or th))

    near = [o for o in everyone if close(*o)]
    same_head = [device_at(*o) for o in everyone if not (o[0] or o[1] or o[2] or o[3])]

    barrier = pltpu.get_barrier_semaphore()
    for o in near:
        pl.semaphore_signal(barrier, inc=1, device_id=device_at(*o), device_id_type=MESH)

    q_copy = pltpu.make_async_copy(
        q_hbm.at[:, pl.ds(pl.multiple_of(head_group * heads * HD, 128), heads * HD)], q_v, in_sem.at[0]
    )
    q_copy.start()
    len_copy = pltpu.make_async_copy(len_hbm, len_ref, small_sem.at[0])
    len_copy.start()
    kv_copies = []
    chunks = kv_sem.shape[0]
    per_chunk = rows // chunks
    for c in range(chunks):
        copy = pltpu.make_async_copy(
            kv_hbm.at[pl.ds(c * per_chunk, per_chunk), 0], kv_v.at[pl.ds(c * per_chunk, per_chunk)], kv_sem.at[c]
        )
        copy.start()
        kv_copies.append(copy)

    ids_copy = pltpu.make_async_copy(ids_hbm, ids_v, small_sem.at[1])
    ids_copy.start()
    gates_copy = pltpu.make_async_copy(gates_hbm, gates_v, small_sem.at[2])
    gates_copy.start()
    gain_copy = pltpu.make_async_copy(gain_hbm, gain_v, small_sem.at[3])
    gain_copy.start()
    ow_copy = pltpu.make_async_copy(ow_hbm, ow_v, in_sem.at[1])
    wgu_copy = pltpu.make_async_copy(wgu_hbm.at[0], wgu_v, in_sem.at[3])
    wd_copy = pltpu.make_async_copy(wd_hbm.at[0], wd_v, in_sem.at[4])
    ow_copy.start()
    res_copy = pltpu.make_async_copy(
        resid_hbm.at[:, pl.ds(pl.multiple_of(member * 128, 128), 128)], res_v, in_sem.at[2]
    )
    res_copy.start()

    ids_copy.wait()
    gates_copy.wait()
    eye = (
        lax.broadcasted_iota(jnp.int32, (TOPK, TOPK), 0) == lax.broadcasted_iota(jnp.int32, (TOPK, TOPK), 1)
    ).astype(BF16)

    def flipped(value):
        return lax.dot_general(value.astype(BF16), eye, (((0,), (0,)), ((), ())), preferred_element_type=F32)

    gates_t = gates_v[...]
    gates_high = gates_t.astype(BF16).astype(F32)
    gates_middle = (gates_t - gates_high).astype(BF16).astype(F32)
    ids = flipped(ids_v[...].astype(F32))
    gates = flipped(gates_high) + (flipped(gates_middle) + flipped(gates_t - gates_high - gates_middle))
    col = lax.broadcasted_iota(jnp.int32, (rows, experts * SLOTS), 1)
    expert = (col // SLOTS).astype(F32)
    hit = jnp.zeros((rows, experts * SLOTS), F32)
    gate_cols = jnp.zeros((rows, experts * SLOTS), F32)
    for k in range(TOPK):
        same = ids[:, k : k + 1] == expert
        hit = jnp.where(same, 1.0, hit)
        gate_cols = jnp.where(same, gates[:, k : k + 1], gate_cols)
    below = (
        lax.broadcasted_iota(jnp.int32, (rows, rows), 1) < lax.broadcasted_iota(jnp.int32, (rows, rows), 0)
    ).astype(BF16)
    rank = jnp.dot(below, hit.astype(BF16), preferred_element_type=F32)
    placed = jnp.where(rank == (col % SLOTS).astype(F32), hit, 0.0)
    same_row = (
        lax.broadcasted_iota(jnp.int32, (rows, rows), 1) == lax.broadcasted_iota(jnp.int32, (rows, rows), 0)
    ).astype(BF16)
    pick[...] = lax.dot_general(
        placed.astype(BF16), same_row, (((0,), (0,)), ((), ())), preferred_element_type=F32
    ).astype(BF16)
    combine = placed * gate_cols
    combine_high = combine.astype(BF16).astype(F32)
    mix[...] = jnp.concatenate([combine_high, combine - combine_high], axis=0).astype(BF16)

    q_copy.wait()
    for j in range(heads):
        qf[j * rows : (j + 1) * rows, :] = q_v[:, j * HD : (j + 1) * HD].astype(F32)
    len_copy.wait()
    first = part * span
    position = first + lax.broadcasted_iota(jnp.int32, (heads, span), 1)
    scale = 1.0 / math.sqrt(HD)

    def attend_scores(batch):
        made = []
        for r in batch:
            query = qf[pl.ds(r, heads, stride=rows), :].astype(BF16)
            made.append(
                lax.dot_general(query, kv_v[r, :, :HD], (((1,), (1,)), ((), ())), preferred_element_type=F32)
            )
        return made

    def attend_values(batch, made):
        valids = [position < len_ref[r] for r in batch]
        made = [jnp.where(valid, score * scale, NEG) for valid, score in zip(valids, made)]
        tops = [jnp.max(score, axis=1, keepdims=True) for score in made]
        weights = [
            jnp.where(valid, jnp.exp(score - top), 0.0) for valid, score, top in zip(valids, made, tops)
        ]
        totals = [jnp.sum(weight, axis=1, keepdims=True) for weight in weights]
        results = [
            jnp.dot(weight.astype(BF16), kv_v[r, :, HD:], preferred_element_type=F32)
            for r, weight in zip(batch, weights)
        ]
        for r, top, total, value in zip(batch, tops, totals, results):
            some = total > 0.0
            safe = jnp.where(some, total, 1.0)
            num[pl.ds(r, heads, stride=rows), :] = value * (1.0 / safe)
            lse[pl.ds(r, heads, stride=rows), :] = jnp.broadcast_to(
                jnp.where(some, top + jnp.log(safe), NEG), (heads, HD)
            )

    batches = [range(c * per_chunk, (c + 1) * per_chunk) for c in range(chunks)]
    ready = None
    for c in range(chunks):
        kv_copies[c].wait()
        made = attend_scores(batches[c])
        if ready is not None:
            attend_values(batches[c - 1], ready)
        ready = made
    attend_values(batches[-1], ready)

    diagonal = lax.broadcasted_iota(jnp.int32, (mine_rows, HD), 0) == lax.broadcasted_iota(
        jnp.int32, (mine_rows, HD), 1
    )
    line = lax.broadcasted_iota(jnp.int32, (8, HD), 0)
    for p in range(parts):
        block = slice(p * mine_rows, (p + 1) * mine_rows)
        a_send[p, :mine_rows, :] = num[block, :].astype(BF16)
        stat = jnp.sum(jnp.where(diagonal, lse[block, :], 0.0), axis=0, keepdims=True)
        high = stat.astype(BF16).astype(F32)
        middle_word = (stat - high).astype(BF16).astype(F32)
        low = stat - high - middle_word
        words = jnp.where(line == 0, high, jnp.where(line == 1, middle_word, jnp.where(line == 2, low, 0.0)))
        a_send[p, mine_rows:, :] = words.astype(BF16)

    pl.semaphore_wait(barrier, len(near))

    def remote(src, dst, sent, received, device):
        return pltpu.make_async_remote_copy(
            src_ref=src,
            dst_ref=dst,
            send_sem=sent,
            recv_sem=received,
            device_id=device,
            device_id_type=MESH,
        )

    for i, device in enumerate(same_head):
        remote(a_send.at[lax.rem(device[2], parts)], a_recv.at[i], send_sem.at[0], recv_sem.at[0], device).start()
    pl.semaphore_signal(hello_sem, inc=1, device_id=device_at(0, 1, 0, 1, 0), device_id_type=MESH)
    done_a = remote(a_send.at[pl.ds(0, parts - 1)], a_recv, send_sem.at[0], recv_sem.at[0], same_head[0])
    for i, block in enumerate(piece_member):
        there = pl.ds(pl.multiple_of(block * 128, 128), 128)
        pltpu.make_async_copy(wgu_hbm.at[0, there, :], wgu_v.at[pl.ds(i * 128, 128), :], in_sem.at[3]).start()
    own = pl.ds(pl.multiple_of(part * mine_rows, 8), mine_rows)
    values = [num[own, :]]
    levels = [lse[own, :][:, 0:1]]
    done_a.wait_recv()
    pl.semaphore_wait(hello_sem, 1)
    for d in range(parts - 1):
        values.append(a_recv[d, :mine_rows, :].astype(F32))
        row = jnp.sum(a_recv[d, mine_rows:, :].astype(F32), axis=0, keepdims=True)
        levels.append(jnp.sum(jnp.where(diagonal, row, 0.0), axis=1, keepdims=True))
    peak = functools.reduce(jnp.maximum, levels)
    shares = [jnp.exp(level - peak) for level in levels]
    whole = functools.reduce(jnp.add, shares)
    merged = functools.reduce(jnp.add, [v * s for v, s in zip(values, shares)]) * (1.0 / whole)
    per_member = mine_rows // rows
    attended = jnp.concatenate(
        [merged[i * rows : (i + 1) * rows, :] for i in range(per_member)], axis=1
    ).astype(BF16)

    ow_copy.wait()
    for band in reversed(bands):
        peers = [(i, o) for i, o in enumerate(row_group) if ring(o[4], parts) == band]
        blocks = [device_at(*o) for _, o in peers]
        pieces = [
            jnp.dot(
                attended,
                ow_v[:, pl.ds(pl.multiple_of((device[0] * tps + device[2]) * 128, 128), 128)],
                preferred_element_type=F32,
            )
            for device in blocks
        ]
        for (i, _), piece in zip(peers, pieces):
            b_send[i, :, :] = piece.astype(BF16)
        for (i, _), device in zip(peers, blocks):
            remote(b_send.at[i], b_recv.at[i], send_sem.at[1], recv_sem.at[1], device).start()
    kept = jnp.dot(
        attended, ow_v[:, pl.ds(pl.multiple_of(member * 128, 128), 128)], preferred_element_type=F32
    )
    done_b = remote(
        b_send.at[pl.ds(0, members - 1)], b_recv, send_sem.at[1], recv_sem.at[1], device_at(*row_group[0])
    )
    for i, block in enumerate(piece_member):
        there = pl.ds(pl.multiple_of(block * 128, 128), 128)
        pltpu.make_async_copy(wd_hbm.at[0, :, there], wd_v.at[:, pl.ds(i * 128, 128)], in_sem.at[4]).start()
    res_copy.wait()
    acc = res_v[...].astype(F32) + kept
    done_b.wait_recv()
    for d in range(members - 1):
        acc = acc + b_recv[d, :, :].astype(F32)
    middle = acc.astype(BF16)

    chosen = jnp.dot(pick[...], middle, preferred_element_type=F32).astype(BF16)
    d_send[...] = chosen.reshape(experts, SLOTS, 128)
    some_device = device_at(*everyone[0])
    for ds, gh, gl, th, tl in everyone:
        device = device_at(ds, gh, gl, th, tl)
        slot = piece_index[ds, th, (parts - tl) % parts] * grps + group_index[gh, (grp_low - gl) % grp_low]
        remote(
            d_send.at[(device[0] * grps + device[1]) * tps + device[2]],
            d_recv.at[slot],
            send_sem.at[2],
            band_sem.at[ring(tl, parts)],
            device,
        ).start()
    d_recv[0, :, :] = d_send[mine_expert, :, :]
    gain_copy.wait()
    wgu_copy.wait()
    both = None
    square = None
    for band in bands:
        members_in = band_pieces[band]
        count = len(members_in) * grps - (1 if band == 0 else 0)
        some = pl.ds(0, count)
        remote(d_recv.at[some], d_recv.at[some], send_sem.at[2], band_sem.at[band], some_device).wait_recv()
        inputs = []
        for i in members_in:
            piece = d_recv[i * grps : (i + 1) * grps, :, :].reshape(grps * SLOTS, 128).astype(F32)
            square = piece * piece if square is None else square + piece * piece
            inputs.append((piece * gain_v[pl.ds(piece_member[i], 1), :]).astype(BF16))
        partial = jnp.dot(
            jnp.concatenate(inputs, axis=1),
            wgu_v[members_in[0] * 128 : (members_in[-1] + 1) * 128, :],
            preferred_element_type=F32,
        )
        both = partial if both is None else both + partial
    done_d = remote(
        d_send.at[pl.ds(0, experts - 1)], d_recv.at[pl.ds(0, experts - 1)], send_sem.at[2], band_sem.at[0], some_device
    )
    inv_rms = lax.rsqrt(jnp.sum(square, axis=1, keepdims=True) * (1.0 / width) + 1e-6)
    both = both * inv_rms
    gate = both[:, :inner]
    act = (gate / (1.0 + jnp.exp(-gate)) * both[:, inner:]).astype(BF16)
    wd_copy.wait()

    for band in reversed(bands):
        low, high = band_pieces[band][0], band_pieces[band][-1] + 1
        produced = jnp.dot(act, wd_v[:, low * 128 : high * 128], preferred_element_type=F32).astype(BF16)
        for p in range(low, high):
            e_send[:, p, :, :] = produced[:, (p - low) * 128 : (p - low + 1) * 128].reshape(grps, SLOTS, 128)
        for ds, gh, gl, th, tl in everyone:
            p = piece_index[ds, th, tl]
            if low <= p < high:
                remote(
                    e_send.at[group_index[gh, gl], p],
                    e_recv.at[mine_expert],
                    send_sem.at[3],
                    recv_sem.at[2],
                    device_at(ds, gh, gl, th, tl),
                ).start()
    e_recv[mine_expert, :, :] = e_send[0, 0, :, :]
    some = pl.ds(0, experts - 1)
    done_e = remote(e_recv.at[some], e_recv.at[some], send_sem.at[3], recv_sem.at[2], some_device)
    done_e.wait_recv()
    returned = e_recv[...].reshape(experts * SLOTS, 128)
    gated = jnp.dot(mix[...], returned, preferred_element_type=F32)
    out_ref[...] = (middle.astype(F32) + (gated[:rows, :] + gated[rows:, :])).astype(BF16)
    for done in (done_a, done_b, done_d, done_e):
        done.wait_send()


def body(queries, kv_cache, lengths, out_weight, resid, norm_gain, expert_ids, expert_gates, w_gate_up, w_down):
    sides, grps, tps = lax.axis_size("side"), lax.axis_size("grp"), lax.axis_size("tp")
    members = sides * tps
    experts = members * grps
    rows = queries.shape[0]
    parts = 4
    heads = 8
    span = kv_cache.shape[2]
    width = out_weight.shape[1]
    mine_rows = rows * heads // parts
    anywhere = pl.BlockSpec(memory_space=pl.ANY)
    return pl.pallas_call(
        functools.partial(kernel, (sides, grps, tps, parts)),
        out_shape=pltpu.VMEM((rows, width // members), BF16),
        in_specs=[anywhere] * 10,
        out_specs=pl.BlockSpec(memory_space=pltpu.VMEM),
        scratch_shapes=[
            pltpu.SMEM((rows,), jnp.int32),
            pltpu.VMEM((members, width // members), F32),
            pltpu.VMEM((TOPK, rows), jnp.int32),
            pltpu.VMEM((TOPK, rows), F32),
            pltpu.VMEM((rows, heads * HD), BF16),
            pltpu.VMEM((rows, span, 2 * HD), BF16),
            pltpu.VMEM(out_weight.shape, BF16),
            pltpu.VMEM((rows, 128), BF16),
            pltpu.VMEM(w_gate_up.shape[1:], BF16),
            pltpu.VMEM(w_down.shape[1:], BF16),
            pltpu.VMEM((rows * heads, HD), F32),
            pltpu.VMEM((rows * heads, HD), F32),
            pltpu.VMEM((rows * heads, HD), F32),
            pltpu.VMEM((experts * SLOTS, rows), BF16),
            pltpu.VMEM((2 * rows, experts * SLOTS), BF16),
            pltpu.VMEM((parts, mine_rows + 8, HD), BF16),
            pltpu.VMEM((parts - 1, mine_rows + 8, HD), BF16),
            pltpu.VMEM((members, rows, 128), BF16),
            pltpu.VMEM((members - 1, rows, 128), BF16),
            pltpu.VMEM((experts, SLOTS, 128), BF16),
            pltpu.VMEM((experts, SLOTS, 128), BF16),
            pltpu.VMEM((grps, members, SLOTS, 128), BF16),
            pltpu.VMEM((experts, SLOTS, 128), BF16),
            pltpu.SemaphoreType.DMA((4,)),
            pltpu.SemaphoreType.DMA((2,)),
            pltpu.SemaphoreType.DMA((5,)),
            pltpu.SemaphoreType.DMA((4,)),
            pltpu.SemaphoreType.DMA((3,)),
            pltpu.SemaphoreType.DMA((3,)),
            pltpu.SemaphoreType.REGULAR,
        ],
        compiler_params=pltpu.CompilerParams(
            collective_id=0, has_side_effects=True, vmem_limit_bytes=56 * 1024 * 1024
        ),
        name="layer",
    )(
        lengths,
        queries,
        kv_cache,
        out_weight,
        resid,
        norm_gain.reshape(members, width // members),
        expert_ids.T,
        expert_gates.T,
        w_gate_up,
        w_down,
    )


def solution(mesh):
    in_specs = (
        P("grp", "side"),
        P("grp", ("side", "tp"), None, None),
        P("grp"),
        P(("side", "tp"), None),
        P("grp", None),
        P(),
        P("grp", None),
        P("grp", None),
        P(("side", "grp", "tp"), None, None),
        P(("side", "grp", "tp"), None, None),
    )
    out_specs = P("grp", ("side", "tp"))
    return jax.shard_map(body, mesh=mesh, in_specs=in_specs, out_specs=out_specs, check_vma=False)
```

```python
import functools
import math

import jax
import jax.numpy as jnp
from jax import lax
from jax.experimental import pallas as pl
from jax.experimental.pallas import tpu as pltpu
from jax.sharding import PartitionSpec as P

HD = 128
TOPK = 8
SLOTS = 4
NEG = -1e30
F32 = jnp.float32
BF16 = jnp.bfloat16
MESH = pl.DeviceIdType.MESH


def kernel(
    dims,
    len_hbm,
    q_hbm,
    kv_hbm,
    ow_hbm,
    resid_hbm,
    gain_hbm,
    ids_hbm,
    gates_hbm,
    wgu_hbm,
    wd_hbm,
    out_ref,
    len_ref,
    gain_v,
    ids_v,
    gates_v,
    q_v,
    kv_v,
    ow_v,
    res_v,
    wgu_v,
    wd_v,
    qf,
    num,
    lse,
    pick,
    mix,
    a_send,
    a_recv,
    b_send,
    b_recv,
    d_send,
    d_recv,
    e_send,
    e_recv,
    small_sem,
    kv_sem,
    in_sem,
    send_sem,
    recv_sem,
    band_sem,
    hello_sem,
):
    sides, grps, tps, parts = dims
    members = sides * tps
    experts = members * grps
    rows = q_v.shape[0]
    heads = q_v.shape[1] // HD
    span = kv_v.shape[1]
    width = ow_v.shape[1]
    mine_rows = rows * heads // parts
    inner = wd_v.shape[0]
    side = lax.axis_index("side")
    grp = lax.axis_index("grp")
    tp = lax.axis_index("tp")
    member = side * tps + tp
    part = lax.rem(tp, parts)
    head_group = tp // parts
    groups = tps // parts
    mine_expert = (side * grps + grp) * tps + tp

    grp_low = 4 if grps % 4 == 0 else grps
    grp_high = grps // grp_low
    side_at = [lax.rem(side + d, sides) for d in range(sides)]
    grp_at = {}
    for hi in range(grp_high):
        for lo in range(grp_low):
            grp_at[hi, lo] = lax.rem(grp // grp_low + hi, grp_high) * grp_low + lax.rem(
                lax.rem(grp, grp_low) + lo, grp_low
            )
    tp_at = {}
    for hi in range(groups):
        for lo in range(parts):
            tp_at[hi, lo] = lax.rem(head_group + hi, groups) * parts + lax.rem(part + lo, parts)

    def ring(d, size):
        return min(d, size - d)

    offsets = []
    for ds in range(sides):
        for gh, gl in grp_at:
            for th, tl in tp_at:
                if ds or gh or gl or th or tl:
                    far = (1 if th else 2 * gh) + ring(gl, grp_low) + ring(tl, parts)
                    offsets.append((-far, ds, gh, gl, th, tl))
    offsets.sort()

    def device_at(ds, gh, gl, th, tl):
        return side_at[ds], grp_at[gh, gl], tp_at[th, tl]

    everyone = [o[1:] for o in offsets]
    row_group = [o for o in everyone if not (o[1] or o[2])]
    piece_order = sorted(
        [(ds, th, tl) for ds in range(sides) for th, tl in tp_at], key=lambda o: (ring(o[2], parts), o)
    )
    group_order = sorted(grp_at)
    piece_index = {o: i for i, o in enumerate(piece_order)}
    group_index = {o: i for i, o in enumerate(group_order)}
    piece_member = [side_at[ds] * tps + tp_at[th, tl] for ds, th, tl in piece_order]
    bands = sorted({ring(o[2], parts) for o in piece_order})
    band_pieces = {b: [i for i, o in enumerate(piece_order) if ring(o[2], parts) == b] for b in bands}

    def close(ds, gh, gl, th, tl):
        if gh:
            return th and not (ds or tl) and gl != grp_low // 2
        if gl:
            return not (ds or th or tl)
        return not (tl and (ds or th))

    near = [o for o in everyone if close(*o)]
    same_head = [device_at(*o) for o in everyone if not (o[0] or o[1] or o[2] or o[3])]

    barrier = pltpu.get_barrier_semaphore()
    for o in near:
        pl.semaphore_signal(barrier, inc=1, device_id=device_at(*o), device_id_type=MESH)

    q_copy = pltpu.make_async_copy(
        q_hbm.at[:, pl.ds(pl.multiple_of(head_group * heads * HD, 128), heads * HD)], q_v, in_sem.at[0]
    )
    q_copy.start()
    len_copy = pltpu.make_async_copy(len_hbm, len_ref, small_sem.at[0])
    len_copy.start()
    kv_copies = []
    chunks = kv_sem.shape[0]
    per_chunk = rows // chunks
    for c in range(chunks):
        copy = pltpu.make_async_copy(
            kv_hbm.at[pl.ds(c * per_chunk, per_chunk), 0], kv_v.at[pl.ds(c * per_chunk, per_chunk)], kv_sem.at[c]
        )
        copy.start()
        kv_copies.append(copy)

    ids_copy = pltpu.make_async_copy(ids_hbm, ids_v, small_sem.at[1])
    ids_copy.start()
    gates_copy = pltpu.make_async_copy(gates_hbm, gates_v, small_sem.at[2])
    gates_copy.start()
    gain_copy = pltpu.make_async_copy(gain_hbm, gain_v, small_sem.at[3])
    gain_copy.start()
    ow_copy = pltpu.make_async_copy(ow_hbm, ow_v, in_sem.at[1])
    wgu_copy = pltpu.make_async_copy(wgu_hbm.at[0], wgu_v, in_sem.at[3])
    wd_copy = pltpu.make_async_copy(wd_hbm.at[0], wd_v, in_sem.at[4])
    ow_copy.start()
    res_copy = pltpu.make_async_copy(
        resid_hbm.at[:, pl.ds(pl.multiple_of(member * 128, 128), 128)], res_v, in_sem.at[2]
    )
    res_copy.start()

    ids_copy.wait()
    gates_copy.wait()
    eye = (
        lax.broadcasted_iota(jnp.int32, (TOPK, TOPK), 0) == lax.broadcasted_iota(jnp.int32, (TOPK, TOPK), 1)
    ).astype(BF16)

    def flipped(value):
        return lax.dot_general(value.astype(BF16), eye, (((0,), (0,)), ((), ())), preferred_element_type=F32)

    gates_t = gates_v[...]
    gates_high = gates_t.astype(BF16).astype(F32)
    gates_middle = (gates_t - gates_high).astype(BF16).astype(F32)
    ids = flipped(ids_v[...].astype(F32))
    gates = flipped(gates_high) + (flipped(gates_middle) + flipped(gates_t - gates_high - gates_middle))
    col = lax.broadcasted_iota(jnp.int32, (rows, experts * SLOTS), 1)
    expert = (col // SLOTS).astype(F32)
    hit = jnp.zeros((rows, experts * SLOTS), F32)
    gate_cols = jnp.zeros((rows, experts * SLOTS), F32)
    for k in range(TOPK):
        same = ids[:, k : k + 1] == expert
        hit = jnp.where(same, 1.0, hit)
        gate_cols = jnp.where(same, gates[:, k : k + 1], gate_cols)
    below = (
        lax.broadcasted_iota(jnp.int32, (rows, rows), 1) < lax.broadcasted_iota(jnp.int32, (rows, rows), 0)
    ).astype(BF16)
    rank = jnp.dot(below, hit.astype(BF16), preferred_element_type=F32)
    placed = jnp.where(rank == (col % SLOTS).astype(F32), hit, 0.0)
    same_row = (
        lax.broadcasted_iota(jnp.int32, (rows, rows), 1) == lax.broadcasted_iota(jnp.int32, (rows, rows), 0)
    ).astype(BF16)
    pick[...] = lax.dot_general(
        placed.astype(BF16), same_row, (((0,), (0,)), ((), ())), preferred_element_type=F32
    ).astype(BF16)
    combine = placed * gate_cols
    combine_high = combine.astype(BF16).astype(F32)
    mix[...] = jnp.concatenate([combine_high, combine - combine_high], axis=0).astype(BF16)

    q_copy.wait()
    for j in range(heads):
        qf[j * rows : (j + 1) * rows, :] = q_v[:, j * HD : (j + 1) * HD].astype(F32)
    len_copy.wait()
    first = part * span
    position = first + lax.broadcasted_iota(jnp.int32, (heads, span), 1)
    scale = 1.0 / math.sqrt(HD)

    def attend_scores(batch):
        made = []
        for r in batch:
            query = qf[pl.ds(r, heads, stride=rows), :].astype(BF16)
            made.append(
                lax.dot_general(query, kv_v[r, :, :HD], (((1,), (1,)), ((), ())), preferred_element_type=F32)
            )
        return made

    def attend_values(batch, made):
        valids = [position < len_ref[r] for r in batch]
        made = [jnp.where(valid, score * scale, NEG) for valid, score in zip(valids, made)]
        tops = [jnp.max(score, axis=1, keepdims=True) for score in made]
        weights = [
            jnp.where(valid, jnp.exp(score - top), 0.0) for valid, score, top in zip(valids, made, tops)
        ]
        totals = [jnp.sum(weight, axis=1, keepdims=True) for weight in weights]
        results = [
            jnp.dot(weight.astype(BF16), kv_v[r, :, HD:], preferred_element_type=F32)
            for r, weight in zip(batch, weights)
        ]
        for r, top, total, value in zip(batch, tops, totals, results):
            some = total > 0.0
            safe = jnp.where(some, total, 1.0)
            num[pl.ds(r, heads, stride=rows), :] = value * (1.0 / safe)
            lse[pl.ds(r, heads, stride=rows), :] = jnp.broadcast_to(
                jnp.where(some, top + jnp.log(safe), NEG), (heads, HD)
            )

    batches = [range(c * per_chunk, (c + 1) * per_chunk) for c in range(chunks)]
    ready = None
    for c in range(chunks):
        kv_copies[c].wait()
        made = attend_scores(batches[c])
        if ready is not None:
            attend_values(batches[c - 1], ready)
        ready = made
    attend_values(batches[-1], ready)

    diagonal = lax.broadcasted_iota(jnp.int32, (mine_rows, HD), 0) == lax.broadcasted_iota(
        jnp.int32, (mine_rows, HD), 1
    )
    line = lax.broadcasted_iota(jnp.int32, (8, HD), 0)
    for p in range(parts):
        block = slice(p * mine_rows, (p + 1) * mine_rows)
        a_send[p, :mine_rows, :] = num[block, :].astype(BF16)
        stat = jnp.sum(jnp.where(diagonal, lse[block, :], 0.0), axis=0, keepdims=True)
        high = stat.astype(BF16).astype(F32)
        middle_word = (stat - high).astype(BF16).astype(F32)
        low = stat - high - middle_word
        words = jnp.where(line == 0, high, jnp.where(line == 1, middle_word, jnp.where(line == 2, low, 0.0)))
        a_send[p, mine_rows:, :] = words.astype(BF16)

    pl.semaphore_wait(barrier, len(near))

    def remote(src, dst, sent, received, device):
        return pltpu.make_async_remote_copy(
            src_ref=src,
            dst_ref=dst,
            send_sem=sent,
            recv_sem=received,
            device_id=device,
            device_id_type=MESH,
        )

    for i, device in enumerate(same_head):
        remote(a_send.at[lax.rem(device[2], parts)], a_recv.at[i], send_sem.at[0], recv_sem.at[0], device).start()
    pl.semaphore_signal(hello_sem, inc=1, device_id=device_at(0, 1, 0, 1, 0), device_id_type=MESH)
    done_a = remote(a_send.at[pl.ds(0, parts - 1)], a_recv, send_sem.at[0], recv_sem.at[0], same_head[0])
    for i, block in enumerate(piece_member):
        there = pl.ds(pl.multiple_of(block * 128, 128), 128)
        pltpu.make_async_copy(wgu_hbm.at[0, there, :], wgu_v.at[pl.ds(i * 128, 128), :], in_sem.at[3]).start()
    own = pl.ds(pl.multiple_of(part * mine_rows, 8), mine_rows)
    values = [num[own, :]]
    levels = [lse[own, :][:, 0:1]]
    done_a.wait_recv()
    pl.semaphore_wait(hello_sem, 1)
    for d in range(parts - 1):
        values.append(a_recv[d, :mine_rows, :].astype(F32))
        row = jnp.sum(a_recv[d, mine_rows:, :].astype(F32), axis=0, keepdims=True)
        levels.append(jnp.sum(jnp.where(diagonal, row, 0.0), axis=1, keepdims=True))
    peak = functools.reduce(jnp.maximum, levels)
    shares = [jnp.exp(level - peak) for level in levels]
    whole = functools.reduce(jnp.add, shares)
    merged = functools.reduce(jnp.add, [v * s for v, s in zip(values, shares)]) * (1.0 / whole)
    per_member = mine_rows // rows
    attended = jnp.concatenate(
        [merged[i * rows : (i + 1) * rows, :] for i in range(per_member)], axis=1
    ).astype(BF16)

    ow_copy.wait()
    for band in reversed(bands):
        peers = [(i, o) for i, o in enumerate(row_group) if ring(o[4], parts) == band]
        blocks = [device_at(*o) for _, o in peers]
        pieces = [
            jnp.dot(
                attended,
                ow_v[:, pl.ds(pl.multiple_of((device[0] * tps + device[2]) * 128, 128), 128)],
                preferred_element_type=F32,
            )
            for device in blocks
        ]
        for (i, _), piece in zip(peers, pieces):
            b_send[i, :, :] = piece.astype(BF16)
        for (i, _), device in zip(peers, blocks):
            remote(b_send.at[i], b_recv.at[i], send_sem.at[1], recv_sem.at[1], device).start()
    kept = jnp.dot(
        attended, ow_v[:, pl.ds(pl.multiple_of(member * 128, 128), 128)], preferred_element_type=F32
    )
    done_b = remote(
        b_send.at[pl.ds(0, members - 1)], b_recv, send_sem.at[1], recv_sem.at[1], device_at(*row_group[0])
    )
    for i, block in enumerate(piece_member):
        there = pl.ds(pl.multiple_of(block * 128, 128), 128)
        pltpu.make_async_copy(wd_hbm.at[0, :, there], wd_v.at[:, pl.ds(i * 128, 128)], in_sem.at[4]).start()
    res_copy.wait()
    acc = res_v[...].astype(F32) + kept
    done_b.wait_recv()
    for d in range(members - 1):
        acc = acc + b_recv[d, :, :].astype(F32)
    middle = acc.astype(BF16)

    chosen = jnp.dot(pick[...], middle, preferred_element_type=F32).astype(BF16)
    d_send[...] = chosen.reshape(experts, SLOTS, 128)
    some_device = device_at(*everyone[0])
    for ds, gh, gl, th, tl in everyone:
        device = device_at(ds, gh, gl, th, tl)
        slot = piece_index[ds, th, (parts - tl) % parts] * grps + group_index[gh, (grp_low - gl) % grp_low]
        remote(
            d_send.at[(device[0] * grps + device[1]) * tps + device[2]],
            d_recv.at[slot],
            send_sem.at[2],
            band_sem.at[ring(tl, parts)],
            device,
        ).start()
    d_recv[0, :, :] = d_send[mine_expert, :, :]
    gain_copy.wait()
    wgu_copy.wait()
    both = None
    square = None
    for band in bands:
        members_in = band_pieces[band]
        count = len(members_in) * grps - (1 if band == 0 else 0)
        some = pl.ds(0, count)
        remote(d_recv.at[some], d_recv.at[some], send_sem.at[2], band_sem.at[band], some_device).wait_recv()
        inputs = []
        for i in members_in:
            piece = d_recv[i * grps : (i + 1) * grps, :, :].reshape(grps * SLOTS, 128).astype(F32)
            square = piece * piece if square is None else square + piece * piece
            inputs.append((piece * gain_v[pl.ds(piece_member[i], 1), :]).astype(BF16))
        partial = jnp.dot(
            jnp.concatenate(inputs, axis=1),
            wgu_v[members_in[0] * 128 : (members_in[-1] + 1) * 128, :],
            preferred_element_type=F32,
        )
        both = partial if both is None else both + partial
    done_d = remote(
        d_send.at[pl.ds(0, experts - 1)], d_recv.at[pl.ds(0, experts - 1)], send_sem.at[2], band_sem.at[0], some_device
    )
    inv_rms = lax.rsqrt(jnp.sum(square, axis=1, keepdims=True) * (1.0 / width) + 1e-6)
    both = both * inv_rms
    gate = both[:, :inner]
    act = (gate / (1.0 + jnp.exp(-gate)) * both[:, inner:]).astype(BF16)
    wd_copy.wait()

    for band in reversed(bands):
        low, high = band_pieces[band][0], band_pieces[band][-1] + 1
        produced = jnp.dot(act, wd_v[:, low * 128 : high * 128], preferred_element_type=F32).astype(BF16)
        for p in range(low, high):
            e_send[:, p, :, :] = produced[:, (p - low) * 128 : (p - low + 1) * 128].reshape(grps, SLOTS, 128)
        for ds, gh, gl, th, tl in everyone:
            p = piece_index[ds, th, tl]
            if low <= p < high:
                remote(
                    e_send.at[group_index[gh, gl], p],
                    e_recv.at[mine_expert],
                    send_sem.at[3],
                    recv_sem.at[2],
                    device_at(ds, gh, gl, th, tl),
                ).start()
    e_recv[mine_expert, :, :] = e_send[0, 0, :, :]
    some = pl.ds(0, experts - 1)
    done_e = remote(e_recv.at[some], e_recv.at[some], send_sem.at[3], recv_sem.at[2], some_device)
    for done in (done_a, done_b, done_d):
        done.wait_send()
    done_e.wait_recv()
    returned = e_recv[...].reshape(experts * SLOTS, 128)
    gated = jnp.dot(mix[...], returned, preferred_element_type=F32)
    out_ref[...] = (middle.astype(F32) + (gated[:rows, :] + gated[rows:, :])).astype(BF16)
    done_e.wait_send()


def body(queries, kv_cache, lengths, out_weight, resid, norm_gain, expert_ids, expert_gates, w_gate_up, w_down):
    sides, grps, tps = lax.axis_size("side"), lax.axis_size("grp"), lax.axis_size("tp")
    members = sides * tps
    experts = members * grps
    rows = queries.shape[0]
    parts = 4
    heads = 8
    span = kv_cache.shape[2]
    width = out_weight.shape[1]
    mine_rows = rows * heads // parts
    anywhere = pl.BlockSpec(memory_space=pl.ANY)
    return pl.pallas_call(
        functools.partial(kernel, (sides, grps, tps, parts)),
        out_shape=pltpu.VMEM((rows, width // members), BF16),
        in_specs=[anywhere] * 10,
        out_specs=pl.BlockSpec(memory_space=pltpu.VMEM),
        scratch_shapes=[
            pltpu.SMEM((rows,), jnp.int32),
            pltpu.VMEM((members, width // members), F32),
            pltpu.VMEM((TOPK, rows), jnp.int32),
            pltpu.VMEM((TOPK, rows), F32),
            pltpu.VMEM((rows, heads * HD), BF16),
            pltpu.VMEM((rows, span, 2 * HD), BF16),
            pltpu.VMEM(out_weight.shape, BF16),
            pltpu.VMEM((rows, 128), BF16),
            pltpu.VMEM(w_gate_up.shape[1:], BF16),
            pltpu.VMEM(w_down.shape[1:], BF16),
            pltpu.VMEM((rows * heads, HD), F32),
            pltpu.VMEM((rows * heads, HD), F32),
            pltpu.VMEM((rows * heads, HD), F32),
            pltpu.VMEM((experts * SLOTS, rows), BF16),
            pltpu.VMEM((2 * rows, experts * SLOTS), BF16),
            pltpu.VMEM((parts, mine_rows + 8, HD), BF16),
            pltpu.VMEM((parts - 1, mine_rows + 8, HD), BF16),
            pltpu.VMEM((members, rows, 128), BF16),
            pltpu.VMEM((members - 1, rows, 128), BF16),
            pltpu.VMEM((experts, SLOTS, 128), BF16),
            pltpu.VMEM((experts, SLOTS, 128), BF16),
            pltpu.VMEM((grps, members, SLOTS, 128), BF16),
            pltpu.VMEM((experts, SLOTS, 128), BF16),
            pltpu.SemaphoreType.DMA((4,)),
            pltpu.SemaphoreType.DMA((3,)),
            pltpu.SemaphoreType.DMA((5,)),
            pltpu.SemaphoreType.DMA((4,)),
            pltpu.SemaphoreType.DMA((3,)),
            pltpu.SemaphoreType.DMA((3,)),
            pltpu.SemaphoreType.REGULAR,
        ],
        compiler_params=pltpu.CompilerParams(
            collective_id=0, has_side_effects=True, vmem_limit_bytes=56 * 1024 * 1024
        ),
        name="layer",
    )(
        lengths,
        queries,
        kv_cache,
        out_weight,
        resid,
        norm_gain.reshape(members, width // members),
        expert_ids.T,
        expert_gates.T,
        w_gate_up,
        w_down,
    )


def solution(mesh):
    in_specs = (
        P("grp", "side"),
        P("grp", ("side", "tp"), None, None),
        P("grp"),
        P(("side", "tp"), None),
        P("grp", None),
        P(),
        P("grp", None),
        P("grp", None),
        P(("side", "grp", "tp"), None, None),
        P(("side", "grp", "tp"), None, None),
    )
    out_specs = P("grp", ("side", "tp"))
    return jax.shard_map(body, mesh=mesh, in_specs=in_specs, out_specs=out_specs, check_vma=False)
```
